256 devices in a mesh: slab: 16 (over x_lo, y, core), chan: 16 (over x_hi, z).
Axes of the slice: x: 4 (x_hi: 2, x_lo: 2; x = x_hi * 2 + x_lo), y: 4, z: 8, core: 2. Of those that a mesh axis runs over, the one named last changes fastest.
Arguments:
- field: bfloat16 [1, 128, 128, 128, 128], P(None, 'chan', 'slab'), may hold values from -6 to 6
- local_weight: bfloat16 [128, 128], replicated, may hold values from -0.5 to 0.5
- bias: float32 [128], replicated, may hold values from -3 to 3
- spec_weight: float32 [2, 128, 128, 4096], P(None, 'chan', None, 'slab'), may hold values from -4.2 to 4.2
Outputs:
- activated: bfloat16 [1, 128, 128, 128, 128], P(None, 'chan', 'slab')
The draws below stay inside these ranges and needn't reach their ends.
All inputs are finite; a program needn't handle non-finite values.
Results may differ from the reference program's by a relative error of at most 0.0026.
Values may be sent and summed in bfloat16 or wider, within the bound.
No kernel may reach another device: no remote copies, remote signals or barrier semaphores. Data moves between devices by JAX's collectives and lax.ppermute only.
A program may use at most 64 MiB of HBM per device.

```python
import math
import jax
import jax.numpy as jnp
from jax import lax

GRID = 128
CHANNELS = 128
KEEP = 16
SAMPLES = 1
MODES = 4096


def block_scale(own_key, shape, pieces, least, top_value):
    loudness = 1.0
    for dim, blocks in pieces:
        draws = jax.random.uniform(jax.random.fold_in(jax.random.fold_in(own_key, 6), dim), (blocks,), jnp.float32, least / len(pieces), top_value / len(pieces))
        loudness = loudness * jnp.repeat(jnp.exp(draws), shape[dim] // blocks).reshape((-1,) + (1,) * (len(shape) - 1 - dim))
    return loudness


def scatter_about(key, shape, scale, most, split=(), kind=jnp.bfloat16):
    entries = jax.random.normal(key, shape, jnp.float32) * scale
    if len(split) > 0:
        entries = block_scale(key, shape, split, -0.22, 0.18) * entries
    return jnp.clip(entries, min=-most, max=most).astype(kind)


def setup_inputs(seed: int = 0) -> dict:
    arg_keys = jax.random.split(jax.random.key(seed), 5)
    field = scatter_about(arg_keys[0], (SAMPLES, CHANNELS, GRID, GRID, GRID), 1.0, 6.0, ((1, 16), (2, 16)))
    local_weight = scatter_about(arg_keys[1], (CHANNELS, CHANNELS), CHANNELS ** -0.5, 0.5)
    bias = scatter_about(arg_keys[2], (CHANNELS,), 0.5, 3.0, (), jnp.float32)
    spec_weight = scatter_about(arg_keys[3], (2, CHANNELS, CHANNELS, MODES), 0.7, 4.2, ((1, 16), (3, 16)), jnp.float32)
    return dict(field=field, local_weight=local_weight, bias=bias, spec_weight=spec_weight)


PRECISE = lax.Precision.HIGHEST


def mode_freqs(count, length):
    index = jnp.arange(count, dtype=jnp.int32)
    return jnp.where(index < count // 2, index, index + (length - count)).astype(jnp.int32)


def phase_table(freqs, positions, length):
    product_int = (freqs[:, None] * positions[None, :]) % length
    return 2.0 * math.pi * product_int.astype(jnp.float32) / length


def build_tables(zcells):
    xfreq = mode_freqs(KEEP, GRID)
    zfreq = jnp.arange(KEEP, dtype=jnp.int32)
    cells = jnp.arange(GRID, dtype=jnp.int32)
    angle_x = phase_table(xfreq, cells, GRID)
    angle_z = phase_table(zfreq, zcells, GRID)
    cos_x, sin_x = jnp.cos(angle_x), jnp.sin(angle_x)
    cos_z, sin_z = jnp.cos(angle_z), jnp.sin(angle_z)
    table_x = jnp.concatenate([cos_x, -sin_x], 0).astype(jnp.bfloat16)
    fold_factor = jnp.where(zfreq == 0, 1.0, 2.0).astype(jnp.float32)
    return cos_x, sin_x, cos_z, sin_z, table_x, fold_factor


def product(form, left, right):
    return jnp.einsum(form, left, right, precision=PRECISE)


def reference(field, local_weight, bias, spec_weight):
    cells = jnp.arange(GRID, dtype=jnp.int32)
    cos_x, sin_x, cos_z, sin_z, table_x, fold_factor = build_tables(cells)
    table_wide = table_x.astype(jnp.float32)
    weight_real, weight_imag = spec_weight[0], spec_weight[1]
    local_wide = local_weight.astype(jnp.float32)

    def one_sample(sample):
        section_x = product("kx,czxy->czky", table_wide, sample.astype(jnp.float32))
        part_real = section_x[:, :, :KEEP]
        part_imag = section_x[:, :, KEEP:]
        wave_real = product("czky,jy->czkj", part_real, cos_x) + product("czky,jy->czkj", part_imag, sin_x)
        wave_imag = product("czky,jy->czkj", part_imag, cos_x) - product("czky,jy->czkj", part_real, sin_x)
        four_real = product("czkj,lz->ckjl", wave_real, cos_z) + product("czkj,lz->ckjl", wave_imag, sin_z)
        four_imag = product("czkj,lz->ckjl", wave_imag, cos_z) - product("czkj,lz->ckjl", wave_real, sin_z)
        coef_real = four_real.reshape(CHANNELS, MODES)
        coef_imag = four_imag.reshape(CHANNELS, MODES)
        mixed_real = product("cm,ocm->om", coef_real, weight_real) - product("cm,ocm->om", coef_imag, weight_imag)
        mixed_imag = product("cm,ocm->om", coef_real, weight_imag) + product("cm,ocm->om", coef_imag, weight_real)
        spectral_real = mixed_real.reshape(CHANNELS, KEEP, KEEP, KEEP) * fold_factor
        spectral_imag = mixed_imag.reshape(CHANNELS, KEEP, KEEP, KEEP) * fold_factor
        plane_real = product("okjl,lz->ozkj", spectral_real, cos_z) - product("okjl,lz->ozkj", spectral_imag, sin_z)
        plane_imag = product("okjl,lz->ozkj", spectral_imag, cos_z) + product("okjl,lz->ozkj", spectral_real, sin_z)
        line_real = product("ozkj,kx->ozxj", plane_real, cos_x) - product("ozkj,kx->ozxj", plane_imag, sin_x)
        line_imag = product("ozkj,kx->ozxj", plane_imag, cos_x) + product("ozkj,kx->ozxj", plane_real, sin_x)

        def one_plane(inputs):
            plane, row_real, row_imag = inputs
            inverse = (product("oxj,jy->oxy", row_real, cos_x) - product("oxj,jy->oxy", row_imag, sin_x)) / (GRID ** 3)
            local = product("oc,cxy->oxy", local_wide, plane.astype(jnp.float32))
            total = inverse + local + bias[:, None, None]
            return jax.nn.gelu(total, approximate=False).astype(jnp.bfloat16)

        planes = lax.map(one_plane, (jnp.moveaxis(sample, 1, 0), jnp.moveaxis(line_real, 1, 0), jnp.moveaxis(line_imag, 1, 0)))
        return jnp.moveaxis(planes, 0, 1)

    return lax.map(one_sample, field)
```

```python
import math

import jax
import jax.numpy as jnp
from jax import lax
from jax.experimental import pallas as pl
from jax.experimental.pallas import tpu as pltpu
from jax.sharding import PartitionSpec as P

GRID = 128
KEEP = 16
BLOCKS = 16
PRECISE = lax.Precision.HIGHEST
SCALE = 2.0**20


def mode_freqs(count, length):
    index = jnp.arange(count, dtype=jnp.int32)
    return jnp.where(index < count // 2, index, index + (length - count))


def phase_table(freqs, positions, length):
    product_int = freqs[:, None] * positions[None, :] % length
    return 2.0 * math.pi * product_int.astype(jnp.float32) / length


def build_tables(zcells):
    xfreq = mode_freqs(KEEP, GRID)
    zfreq = jnp.arange(KEEP, dtype=jnp.int32)
    cells = jnp.arange(GRID, dtype=jnp.int32)
    angle_x = phase_table(xfreq, cells, GRID)
    angle_z = phase_table(zfreq, zcells, GRID)
    cos_x, sin_x = (jnp.cos(angle_x), jnp.sin(angle_x))
    cos_z, sin_z = (jnp.cos(angle_z), jnp.sin(angle_z))
    fold_factor = jnp.where(zfreq == 0, 1.0, 2.0).astype(jnp.float32)
    return (cos_x, sin_x, cos_z, sin_z, fold_factor)


def product(form, left, right):
    return jnp.einsum(form, left, right, precision=PRECISE)


def exact_dot(left, right):
    return jnp.dot(left, right, precision=PRECISE, preferred_element_type=jnp.float32)


def slab_perm(dx, dy, dc):
    pairs = []
    for a in range(2):
        for b in range(4):
            for c in range(2):
                pairs.append(((a * 4 + b) * 2 + c, ((a ^ dx) * 4 + (b ^ dy)) * 2 + (c ^ dc)))
    return pairs


def halve(value, axis, bit, perm):
    own = lax.dynamic_index_in_dim(value, bit, axis, keepdims=False)
    other = lax.dynamic_index_in_dim(value, 1 - bit, axis, keepdims=False)
    return own + lax.ppermute(other, "slab", perm)


def slab_sum(partial):
    me = lax.axis_index("slab")
    rest = partial.shape[1:]
    value = partial.reshape(2, 2, 2, 2, *rest)
    value = halve(value, 3, me % 2, slab_perm(0, 0, 1))
    value = halve(value, 1, me // 4 % 2, slab_perm(0, 2, 0))
    value = halve(value, 1, me // 2 % 2, slab_perm(0, 1, 0))
    return halve(value, 0, me // 8, slab_perm(1, 0, 0))


def map_kernel(weight_ref, cells_ref, out_ref, hold_ref):
    rows = cells_ref.shape[1]
    for x in range(rows):
        block = cells_ref[:, x].reshape(128, 128)
        mapped = jnp.dot(weight_ref[...], block, preferred_element_type=jnp.float32) * SCALE
        square = mapped * mapped
        hold_ref[:, x, :] = mapped * jnp.abs(mapped) * square
    out_ref[...] = hold_ref[...].reshape(out_ref.shape).astype(jnp.bfloat16)


def pointwise_map(weight, cells):
    rows = 16
    return pl.pallas_call(
        map_kernel,
        out_shape=jax.ShapeDtypeStruct((BLOCKS, 8, 64, 128), jnp.bfloat16),
        grid=(64 // rows,),
        in_specs=[
            pl.BlockSpec((128, 128), lambda i: (0, 0)),
            pl.BlockSpec((BLOCKS, rows, 8, 128), lambda i: (0, i, 0, 0)),
        ],
        out_specs=pl.BlockSpec((BLOCKS, 8, rows, 128), lambda i: (0, 0, i, 0)),
        scratch_shapes=[pltpu.VMEM((128, rows, 128), jnp.float32)],
        name="pointwise_map",
    )(weight, cells)


def inverse_kernel(spec_ref, table_z_ref, table_x_ref, table_y_ref, out_ref, plane_ref, line_ref):
    real = exact_dot(spec_ref[:, 0].reshape(128, 256), table_z_ref[...])
    imag = exact_dot(spec_ref[:, 1].reshape(128, 256), table_z_ref[...])
    plane_ref[:16] = (real[:, :128] - imag[:, 128:]).reshape(16, 8, 128)
    plane_ref[16:] = (imag[:, :128] + real[:, 128:]).reshape(16, 8, 128)
    for o in range(8):
        line = exact_dot(table_x_ref[...], plane_ref[:, o, :])
        line_ref[pl.ds(o * 128, 128), :128] = line[:128]
        line_ref[pl.ds(o * 128, 128), 128:] = line[128:]
    for z in range(0, 8, 2):
        field = exact_dot(line_ref[...], table_y_ref[:, z * 128 : (z + 2) * 128])
        out_ref[:, z] = field[:, :128].reshape(8, 128, 128)
        out_ref[:, z + 1] = field[:, 128:].reshape(8, 128, 128)


def inverse_transform(spectrum, cos_x, sin_x, cos_z, sin_z, fold_factor):
    eye_k = jnp.eye(KEEP, dtype=jnp.float32)
    eye_z = jnp.eye(8, dtype=jnp.float32)
    weight = fold_factor / GRID**3
    waves_z = jnp.stack([cos_z, sin_z], 0) * weight[None, :, None]
    table_z = (eye_k[:, None, None, None, :] * waves_z.transpose(1, 0, 2)[None, :, :, :, None]).reshape(256, 256)
    table_x = jnp.concatenate(
        [
            jnp.concatenate([cos_x.T, -sin_x.T], 1),
            jnp.concatenate([sin_x.T, cos_x.T], 1),
        ],
        0,
    )
    waves_y = jnp.stack([cos_x, -sin_x], 0)
    table_y = (eye_z[None, :, None, :, None] * waves_y[:, None, :, None, :]).reshape(256, 1024)
    return pl.pallas_call(
        inverse_kernel,
        out_shape=jax.ShapeDtypeStruct((8, 8, 128, 128), jnp.float32),
        scratch_shapes=[pltpu.VMEM((32, 8, 128), jnp.float32), pltpu.VMEM((1024, 256), jnp.float32)],
        name="inverse_transform",
    )(spectrum, table_z, table_x, table_y)


def finish_kernel(bias_ref, coded_ref, inverse_ref, out_ref):
    coded = coded_ref[0].astype(jnp.float32)
    size = lax.rsqrt(lax.rsqrt(jnp.abs(coded))) * (1.0 / SCALE)
    local = jnp.where(coded < 0, -size, size)
    for o in range(8):
        total = local[o] + inverse_ref[o, 0] + bias_ref[o]
        active = 0.5 * total * (1.0 + lax.erf(total * math.sqrt(0.5)))
        out_ref[o, 0] = active.astype(jnp.bfloat16)


def finish(bias, coded, inverse):
    return pl.pallas_call(
        finish_kernel,
        out_shape=jax.ShapeDtypeStruct((8, 8, 128, 128), jnp.bfloat16),
        grid=(BLOCKS,),
        in_specs=[
            pl.BlockSpec(memory_space=pltpu.SMEM),
            pl.BlockSpec((1, 8, 64, 128), lambda p: (p, 0, 0, 0)),
            pl.BlockSpec((8, 1, 64, 128), lambda p: (0, p // 2, p % 2, 0)),
        ],
        out_specs=pl.BlockSpec((8, 1, 64, 128), lambda p: (0, p // 2, p % 2, 0)),
        name="finish",
    )(bias, coded, inverse)


def forward_transform(field, cos_x, sin_x, cos_z, sin_z):
    table_x = jnp.concatenate([cos_x, -sin_x], 0).astype(jnp.bfloat16)
    section_x = jnp.einsum("kx,czxy->czky", table_x, field, preferred_element_type=jnp.float32)
    part_real = section_x[:, :, :KEEP]
    part_imag = section_x[:, :, KEEP:]
    wave_real = product("czky,jy->czkj", part_real, cos_x) + product("czky,jy->czkj", part_imag, sin_x)
    wave_imag = product("czky,jy->czkj", part_imag, cos_x) - product("czky,jy->czkj", part_real, sin_x)
    four_real = product("czkj,lz->kcjl", wave_real, cos_z) + product("czkj,lz->kcjl", wave_imag, sin_z)
    four_imag = product("czkj,lz->kcjl", wave_imag, cos_z) - product("czkj,lz->kcjl", wave_real, sin_z)
    return jnp.stack([four_real.reshape(KEEP, 8, 256), four_imag.reshape(KEEP, 8, 256)], 1)


def mix(coef, spec_weight):
    real = coef[:, 0].reshape(128, 256)
    imag = coef[:, 1].reshape(128, 256)
    weight_real, weight_imag = spec_weight[0], spec_weight[1]
    mixed_real = jnp.sum(real * weight_real - imag * weight_imag, 1)
    mixed_imag = jnp.sum(real * weight_imag + imag * weight_real, 1)
    return jnp.stack([mixed_real, mixed_imag], 0)


def on_device(field, local_weight, bias, spec_weight):
    chan_local, zdepth = (field.shape[1], field.shape[2])
    zcells = lax.axis_index("slab") * zdepth + jnp.arange(zdepth, dtype=jnp.int32)
    cos_x, sin_x, cos_z, sin_z, fold_factor = build_tables(zcells)
    planes = field[0]
    cells = planes.transpose(1, 2, 0, 3).reshape(BLOCKS, 64, 8, 128)
    cells = lax.all_to_all(cells, "chan", 0, 0, tiled=True)
    partial = forward_transform(planes, cos_x, sin_x, cos_z, sin_z)
    owned = slab_sum(partial)
    spread = lax.optimization_barrier(jnp.broadcast_to(owned[None], (BLOCKS, 2, 8, 256)))
    coef = lax.all_to_all(spread, "chan", 0, 0, tiled=True)
    coded = pointwise_map(local_weight, cells)
    coded = lax.all_to_all(coded, "chan", 0, 0, tiled=True)
    mixed = mix(coef, spec_weight)
    spectrum = lax.all_gather(mixed, "slab", axis=0)
    inverse = inverse_transform(spectrum, cos_x, sin_x, cos_z, sin_z, fold_factor)
    offset = lax.dynamic_slice_in_dim(bias, lax.axis_index("chan") * chan_local, chan_local, 0)
    return finish(offset, coded, inverse)[None]


def solution(mesh):
    placed = (P(None, "chan", "slab", None, None), P(), P(), P(None, "chan", None, "slab"))
    return jax.shard_map(
        on_device,
        mesh=mesh,
        in_specs=placed,
        out_specs=P(None, "chan", "slab", None, None),
        check_vma=False,
    )
```

```python
import math

import jax
import jax.numpy as jnp
from jax import lax
from jax.experimental import pallas as pl
from jax.experimental.pallas import tpu as pltpu
from jax.sharding import PartitionSpec as P


GRID = 128
KEEP = 16
BLOCKS = 16
PRECISE = lax.Precision.HIGHEST
SCALE = 2.0**20
TAIL = (
    -0.9999999035727548,
    -1.1511097265121628,
    -0.4591722285969747,
    -0.05260302599382617,
    0.007216363464760431,
    -0.0002534202677215224,
    -0.0001380938713349715,
    2.9273017695886588e-05,
    -1.9919727297239597e-06,
)


def mode_freqs(count, length):
    index = jnp.arange(count, dtype=jnp.int32)
    return jnp.where(index < count // 2, index, index + (length - count))


def phase_table(freqs, positions, length):
    product_int = freqs[:, None] * positions[None, :] % length
    return 2.0 * math.pi * product_int.astype(jnp.float32) / length


def build_tables(zcells):
    xfreq = mode_freqs(KEEP, GRID)
    zfreq = jnp.arange(KEEP, dtype=jnp.int32)
    cells = jnp.arange(GRID, dtype=jnp.int32)
    angle_x = phase_table(xfreq, cells, GRID)
    angle_z = phase_table(zfreq, zcells, GRID)
    cos_x, sin_x = (jnp.cos(angle_x), jnp.sin(angle_x))
    cos_z, sin_z = (jnp.cos(angle_z), jnp.sin(angle_z))
    fold_factor = jnp.where(zfreq == 0, 1.0, 2.0).astype(jnp.float32)
    return (cos_x, sin_x, cos_z, sin_z, fold_factor)


def product(form, left, right):
    return jnp.einsum(form, left, right, precision=PRECISE)


def exact_dot(left, right):
    return jnp.dot(left, right, precision=PRECISE, preferred_element_type=jnp.float32)


def slab_perm(dx, dy, dc):
    pairs = []
    for a in range(2):
        for b in range(4):
            for c in range(2):
                pairs.append(((a * 4 + b) * 2 + c, ((a ^ dx) * 4 + (b ^ dy)) * 2 + (c ^ dc)))
    return pairs


def halve(value, axis, bit, perm):
    own = lax.dynamic_index_in_dim(value, bit, axis, keepdims=False)
    other = lax.dynamic_index_in_dim(value, 1 - bit, axis, keepdims=False)
    return own + lax.ppermute(other, "slab", perm)


def slab_sum(partial):
    me = lax.axis_index("slab")
    rest = partial.shape[1:]
    value = partial.reshape(2, 2, 2, 2, *rest)
    value = halve(value, 3, me % 2, slab_perm(0, 0, 1))
    value = halve(value, 1, me // 4 % 2, slab_perm(0, 2, 0))
    value = halve(value, 1, me // 2 % 2, slab_perm(0, 1, 0))
    return halve(value, 0, me // 8, slab_perm(1, 0, 0))


def map_kernel(weight_ref, cells_ref, out_ref):
    rows = cells_ref.shape[1]
    for first in range(0, rows, 8):
        coded = []
        for x in range(first, first + 8):
            block = cells_ref[:, x].reshape(128, 128)
            mapped = jnp.dot(weight_ref[...], block, preferred_element_type=jnp.float32) * SCALE
            coded.append(mapped * jnp.abs(mapped) * (mapped * mapped))
        turned = jnp.stack(coded, 0).transpose(1, 0, 2)
        out_ref[:, :, pl.ds(first, 8), :] = turned.reshape(BLOCKS, 8, 8, 128).astype(jnp.bfloat16)


def pointwise_map(weight, cells):
    rows = 16
    return pl.pallas_call(
        map_kernel,
        out_shape=jax.ShapeDtypeStruct((BLOCKS, 8, 64, 128), jnp.bfloat16),
        grid=(64 // rows,),
        in_specs=[
            pl.BlockSpec((128, 128), lambda i: (0, 0)),
            pl.BlockSpec((BLOCKS, rows, 8, 128), lambda i: (0, i, 0, 0)),
        ],
        out_specs=pl.BlockSpec((BLOCKS, 8, rows, 128), lambda i: (0, 0, i, 0)),
        name="pointwise_map",
    )(weight, cells)


def inverse_kernel(spec_ref, table_z_ref, table_x_ref, table_y_ref, out_ref, plane_ref, line_ref):
    real = exact_dot(spec_ref[:, 0].reshape(128, 256), table_z_ref[...])
    imag = exact_dot(spec_ref[:, 1].reshape(128, 256), table_z_ref[...])
    plane_ref[:16] = (real[:, :128] - imag[:, 128:]).reshape(16, 8, 128)
    plane_ref[16:] = (imag[:, :128] + real[:, 128:]).reshape(16, 8, 128)
    for o in range(8):
        line = exact_dot(table_x_ref[...], plane_ref[:, o, :])
        line_ref[pl.ds(o * 128, 128), :128] = line[:128]
        line_ref[pl.ds(o * 128, 128), 128:] = line[128:]
    for z in range(0, 8, 2):
        field = exact_dot(line_ref[...], table_y_ref[:, z * 128 : (z + 2) * 128])
        out_ref[:, z] = field[:, :128].reshape(8, 128, 128)
        out_ref[:, z + 1] = field[:, 128:].reshape(8, 128, 128)


def inverse_transform(spectrum, cos_x, sin_x, cos_z, sin_z, fold_factor):
    eye_k = jnp.eye(KEEP, dtype=jnp.float32)
    eye_z = jnp.eye(8, dtype=jnp.float32)
    weight = fold_factor / GRID**3
    waves_z = jnp.stack([cos_z, sin_z], 0) * weight[None, :, None]
    table_z = (eye_k[:, None, None, None, :] * waves_z.transpose(1, 0, 2)[None, :, :, :, None]).reshape(256, 256)
    table_x = jnp.concatenate(
        [
            jnp.concatenate([cos_x.T, -sin_x.T], 1),
            jnp.concatenate([sin_x.T, cos_x.T], 1),
        ],
        0,
    )
    waves_y = jnp.stack([cos_x, -sin_x], 0)
    table_y = (eye_z[None, :, None, :, None] * waves_y[:, None, :, None, :]).reshape(256, 1024)
    return pl.pallas_call(
        inverse_kernel,
        out_shape=jax.ShapeDtypeStruct((8, 8, 128, 128), jnp.float32),
        scratch_shapes=[pltpu.VMEM((32, 8, 128), jnp.float32), pltpu.VMEM((1024, 256), jnp.float32)],
        name="inverse_transform",
    )(spectrum, table_z, table_x, table_y)


def finish_kernel(bias_ref, coded_ref, inverse_ref, out_ref):
    depth = inverse_ref.shape[1]
    for o in range(8):
        for z in range(depth):
            for half in range(2):
                coded = coded_ref[z * 2 + half, o].astype(jnp.float32)
                size = lax.rsqrt(lax.rsqrt(jnp.abs(coded))) * (1.0 / SCALE)
                local = jnp.where(coded < 0, -size, size)
                rows = pl.ds(half * 64, 64)
                total = local + (inverse_ref[o, z, rows, :] + bias_ref[o])
                size = jnp.abs(total)
                power = TAIL[-1]
                for factor in TAIL[-2::-1]:
                    power = power * size + factor
                active = jnp.maximum(total, 0.0) - size * jnp.exp2(power)
                out_ref[o, z, rows, :] = active.astype(jnp.bfloat16)


def finish(bias, coded, inverse):
    depth = 2
    return pl.pallas_call(
        finish_kernel,
        out_shape=jax.ShapeDtypeStruct((8, 8, 128, 128), jnp.bfloat16),
        grid=(8 // depth,),
        in_specs=[
            pl.BlockSpec(memory_space=pltpu.SMEM),
            pl.BlockSpec((2 * depth, 8, 64, 128), lambda z: (z, 0, 0, 0)),
            pl.BlockSpec((8, depth, 128, 128), lambda z: (0, z, 0, 0)),
        ],
        out_specs=pl.BlockSpec((8, depth, 128, 128), lambda z: (0, z, 0, 0)),
        name="finish",
    )(bias, coded, inverse)


def forward_transform(field, cos_x, sin_x, cos_z, sin_z):
    table_x = jnp.concatenate([cos_x, -sin_x], 0).astype(jnp.bfloat16)
    section_x = jnp.einsum("kx,czxy->czky", table_x, field, preferred_element_type=jnp.float32)
    part_real = section_x[:, :, :KEEP]
    part_imag = section_x[:, :, KEEP:]
    wave_real = product("czky,jy->czkj", part_real, cos_x) + product("czky,jy->czkj", part_imag, sin_x)
    wave_imag = product("czky,jy->czkj", part_imag, cos_x) - product("czky,jy->czkj", part_real, sin_x)
    four_real = product("czkj,lz->kcjl", wave_real, cos_z) + product("czkj,lz->kcjl", wave_imag, sin_z)
    four_imag = product("czkj,lz->kcjl", wave_imag, cos_z) - product("czkj,lz->kcjl", wave_real, sin_z)
    return jnp.stack([four_real.reshape(KEEP, 8, 256), four_imag.reshape(KEEP, 8, 256)], 1)


def chan_perm(dx, dz):
    return [(h * 8 + z, (h ^ dx) * 8 + (z + dz) % 8) for h in range(2) for z in range(8)]


def coef_gather(owned):
    other = lax.ppermute(owned, "chan", chan_perm(1, 0))
    first = lax.axis_index("chan") < 8
    pair = jnp.stack([jnp.where(first, owned, other), jnp.where(first, other, owned)], 0)
    return [pair] + [lax.ppermute(pair, "chan", chan_perm(0, k)) for k in range(1, 8)]


def mix_kernel(place_ref, *refs):
    coefs, weight_ref, out_ref = refs[:8], refs[8], refs[9]
    zpos = place_ref[0]
    for o in range(8):
        real = jnp.zeros((8, 256), jnp.float32)
        imag = jnp.zeros((8, 256), jnp.float32)
        for k in range(8):
            source = lax.rem(zpos + (8 - k), 8)
            for h in range(2):
                rows = pl.ds(pl.multiple_of(h * 64 + source * 8, 8), 8)
                weight_real = weight_ref[0, o, rows, :]
                weight_imag = weight_ref[1, o, rows, :]
                coef_real = coefs[k][h, 0]
                coef_imag = coefs[k][h, 1]
                real += coef_real * weight_real - coef_imag * weight_imag
                imag += coef_real * weight_imag + coef_imag * weight_real
        out_ref[0, pl.ds(o, 1), :] = jnp.sum(real, 0, keepdims=True)
        out_ref[1, pl.ds(o, 1), :] = jnp.sum(imag, 0, keepdims=True)


def mix(coefs, spec_weight):
    place = jnp.reshape(lax.axis_index("chan") % 8, (1,)).astype(jnp.int32)
    whole = pl.BlockSpec(memory_space=pltpu.VMEM)
    return pl.pallas_call(
        mix_kernel,
        out_shape=jax.ShapeDtypeStruct((2, 8, 256), jnp.float32),
        in_specs=[pl.BlockSpec(memory_space=pltpu.SMEM)] + [whole] * 9,
        out_specs=whole,
        name="mix",
    )(place, *coefs, spec_weight)


def on_device(field, local_weight, bias, spec_weight):
    chan_local, zdepth = (field.shape[1], field.shape[2])
    zcells = lax.axis_index("slab") * zdepth + jnp.arange(zdepth, dtype=jnp.int32)
    cos_x, sin_x, cos_z, sin_z, fold_factor = build_tables(zcells)
    planes = field[0]
    cells = planes.transpose(1, 2, 0, 3).reshape(BLOCKS, 64, 8, 128)
    cells = lax.all_to_all(cells, "chan", 0, 0, tiled=True)
    partial = forward_transform(planes, cos_x, sin_x, cos_z, sin_z)
    owned = slab_sum(partial)
    coef = coef_gather(owned)
    coded = pointwise_map(local_weight, cells)
    coded = lax.all_to_all(coded, "chan", 0, 0, tiled=True)
    mixed = mix(coef, spec_weight)
    spectrum = lax.all_gather(mixed, "slab", axis=0)
    inverse = inverse_transform(spectrum, cos_x, sin_x, cos_z, sin_z, fold_factor)
    offset = lax.dynamic_slice_in_dim(bias, lax.axis_index("chan") * chan_local, chan_local, 0)
    return finish(offset, coded, inverse)[None]


def solution(mesh):
    placed = (P(None, "chan", "slab", None, None), P(), P(), P(None, "chan", None, "slab"))
    return jax.shard_map(
        on_device,
        mesh=mesh,
        in_specs=placed,
        out_specs=P(None, "chan", "slab", None, None),
        check_vma=False,
    )
```

```python
import math

import jax
import jax.numpy as jnp
import numpy as np
from jax import lax
from jax.experimental import pallas as pl
from jax.experimental.pallas import tpu as pltpu
from jax.sharding import PartitionSpec as P


GRID = 128
KEEP = 16
BLOCKS = 16
PRECISE = lax.Precision.HIGHEST
CELL_SCALE = 2.0**20
COEF_SCALE = 2.0**6
WHOLE = pl.BlockSpec(memory_space=pltpu.VMEM)
SCALARS = pl.BlockSpec(memory_space=pltpu.SMEM)


def waves(freqs, positions):
    angle = 2.0 * math.pi * (freqs * positions % GRID).astype(np.float32) / np.float32(GRID)
    return np.cos(angle).astype(np.float32), np.sin(angle).astype(np.float32)


def plane_waves():
    index = np.arange(KEEP)
    freqs = np.where(index < KEEP // 2, index, index + GRID - KEEP)
    return waves(freqs[:, None], np.arange(GRID)[None, :])


def depth_angle(first_cell, shape, mode, cell):
    row = lax.broadcasted_iota(jnp.int32, shape, 0)
    lane = lax.broadcasted_iota(jnp.int32, shape, 1)
    turns = mode(row, lane) * (first_cell + cell(row, lane)) % GRID
    return 2.0 * math.pi * turns.astype(jnp.float32) / GRID, row, lane


def exact_dot(left, right):
    return jnp.dot(left, right, precision=PRECISE, preferred_element_type=jnp.float32)


def split(value):
    high = value.astype(jnp.bfloat16)
    return high, (value - high.astype(jnp.float32)).astype(jnp.bfloat16)


def encode(value, scale):
    value = value * scale
    return (value * jnp.abs(value) * (value * value)).astype(jnp.bfloat16)


def decode(coded, scale):
    coded = coded.astype(jnp.float32)
    size = lax.rsqrt(lax.rsqrt(jnp.abs(coded)))
    if scale != 1.0:
        size = size * (1.0 / scale)
    return jnp.where(coded < 0, -size, size)


def slab_perm(dx, dy, dc):
    pairs = []
    for a in range(2):
        for b in range(4):
            for c in range(2):
                pairs.append(((a * 4 + b) * 2 + c, ((a ^ dx) * 4 + (b ^ dy)) * 2 + (c ^ dc)))
    return pairs


def chan_perm(dx, dz):
    return [(h * 8 + z, (h ^ dx) * 8 + (z + dz) % 8) for h in range(2) for z in range(8)]


def halve(value, axis, bit, perm):
    own = lax.dynamic_index_in_dim(value, bit, axis, keepdims=False)
    other = lax.dynamic_index_in_dim(value, 1 - bit, axis, keepdims=False)
    return own + lax.ppermute(other, "slab", perm)


def slab_sum(partial):
    me = lax.axis_index("slab")
    value = partial.reshape(2, 2, 2, 2, *partial.shape[1:])
    value = halve(value, 3, me % 2, slab_perm(0, 0, 1))
    value = halve(value, 1, me // 4 % 2, slab_perm(0, 2, 0))
    value = halve(value, 1, me // 2 % 2, slab_perm(0, 1, 0))
    return halve(value, 0, me // 8, slab_perm(1, 0, 0))


def slab_gather(value):
    value = value[None]
    for step in ((1, 0, 0), (0, 1, 0), (0, 2, 0), (0, 0, 1)):
        value = jnp.concatenate([value, lax.ppermute(value, "slab", slab_perm(*step))], 0)
    return value


MIXED = tuple((e & 1) * 8 | (e >> 1 & 1) * 2 | (e >> 2 & 1) * 4 | e >> 3 for e in range(16))


def forward_kernel(field_ref, table_x_ref, table_y_ref, depth_ref, out_ref, wave_ref, table_z_ref):
    table_y = table_y_ref[...]
    lane = lax.broadcasted_iota(jnp.int32, (KEEP, 512), 1)
    row = lax.broadcasted_iota(jnp.int32, (KEEP, 512), 0)
    same_mode = lane // KEEP % KEEP == row
    for z in range(8):
        sections = []
        for c in range(8):
            section = jnp.dot(table_x_ref[...], field_ref[c, z], preferred_element_type=jnp.float32)
            sections.append(jnp.concatenate([section[:KEEP], section[KEEP:]], 1))
        wave_ref[:, pl.ds(z * 32, 32)] = exact_dot(jnp.concatenate(sections, 0), table_y)
        for part in range(2):
            rows = pl.ds(z * 32 + part * KEEP, KEEP)
            depth = jnp.broadcast_to(depth_ref[pl.ds(z * 2 + part, 1), :], (KEEP, 512))
            table_z_ref[rows, :] = jnp.where(same_mode, depth, 0.0)
    coefs = exact_dot(wave_ref[...], table_z_ref[...]).reshape(8, KEEP, 512).transpose(1, 0, 2)
    out_ref[:, 0] = coefs[:, :, :256]
    out_ref[:, 1] = coefs[:, :, 256:]


def forward_transform(field, first_cell):
    cos_x, sin_x = plane_waves()
    table_x = jnp.asarray(np.concatenate([cos_x, -sin_x], 0)).astype(jnp.bfloat16)
    table_y = jnp.asarray(
        np.concatenate([np.concatenate([cos_x.T, -sin_x.T], 1), np.concatenate([sin_x.T, cos_x.T], 1)], 0)
    )
    angle, row, lane = depth_angle(first_cell, (16, 512), lambda r, n: n % 16, lambda r, n: r // 2)
    from_part, to_part = row % 2, lane // 256
    turned = jnp.where(from_part == 1, jnp.sin(angle), -jnp.sin(angle))
    depth = jnp.where(from_part == to_part, jnp.cos(angle), turned)
    return pl.pallas_call(
        forward_kernel,
        out_shape=jax.ShapeDtypeStruct((KEEP, 2, 8, 256), jnp.float32),
        in_specs=[WHOLE] * 4,
        out_specs=WHOLE,
        scratch_shapes=[pltpu.VMEM((128, 256), jnp.float32), pltpu.VMEM((256, 512), jnp.float32)],
        cost_estimate=pl.CostEstimate(flops=200_000_000, bytes_accessed=3_000_000, transcendentals=0),
        compiler_params=pltpu.CompilerParams(vmem_limit_bytes=12 << 20),
        name="forward_transform",
    )(field, table_x, table_y, depth)


def cut_kernel(field_ref, out_ref, block_ref, turned_ref, fetched, stored):
    parts = fetched.shape[0]
    span = BLOCKS // parts
    fetches, stores = [], []
    for part in range(parts):
        blocks = pl.ds(part * span, span)
        fetches.append(pltpu.make_async_copy(field_ref.at[:, blocks], block_ref.at[:, blocks], fetched.at[part]))
        fetches[part].start()
    for part in range(parts):
        fetches[part].wait()
        for p in range(part * span, (part + 1) * span):
            block = block_ref[:, p].astype(jnp.float32)
            turned_ref[p] = block.transpose(1, 0, 2).astype(jnp.bfloat16)
        blocks = pl.ds(part * span, span)
        stores.append(pltpu.make_async_copy(turned_ref.at[blocks], out_ref.at[blocks], stored.at[part]))
        stores[part].start()
    for store in stores:
        store.wait()


def cut(blocks):
    parts = 8
    in_place = pl.BlockSpec(memory_space=pltpu.HBM)
    return pl.pallas_call(
        cut_kernel,
        out_shape=pltpu.HBM((BLOCKS, 64, 8, 128), jnp.bfloat16),
        in_specs=[in_place],
        out_specs=in_place,
        scratch_shapes=[
            pltpu.VMEM((8, BLOCKS, 64, 128), jnp.bfloat16),
            pltpu.VMEM((BLOCKS, 64, 8, 128), jnp.bfloat16),
            pltpu.SemaphoreType.DMA((parts,)),
            pltpu.SemaphoreType.DMA((parts,)),
        ],
        cost_estimate=pl.CostEstimate(flops=1_000_000, bytes_accessed=4_000_000, transcendentals=0),
        compiler_params=pltpu.CompilerParams(vmem_limit_bytes=60 << 20),
        name="cut",
    )(blocks)


def map_kernel(weight_ref, cells_ref, out_ref, kept_ref, block_ref, held_ref, fetched, stored):
    del kept_ref
    parts = fetched.shape[0]
    rows = 64 // parts
    fetches, stores = [], []
    for part in range(parts):
        span = pl.ds(part * rows, rows)
        fetches.append(pltpu.make_async_copy(cells_ref.at[:, span], block_ref.at[:, span], fetched.at[part]))
        fetches[part].start()
    for part in range(parts):
        fetches[part].wait()
        for first in range(part * rows, (part + 1) * rows, 8):
            coded = []
            for x in range(first, first + 8, 2):
                pair = [block_ref[:, x + near].reshape(128, 128) for near in range(2)]
                mapped = jnp.dot(weight_ref[...], jnp.concatenate(pair, 1), preferred_element_type=jnp.float32)
                mapped = mapped * jnp.abs(mapped) * (mapped * mapped)
                coded += [mapped[:, :128], mapped[:, 128:]]
            turned = jnp.stack(coded, 0).transpose(1, 0, 2)
            held_ref[:, :, pl.ds(first, 8), :] = turned.reshape(BLOCKS, 8, 8, 128).astype(jnp.bfloat16)
        span = pl.ds(part * rows, rows)
        stores.append(
            pltpu.make_async_copy(held_ref.at[:, :, span, :], out_ref.at[:, :, span, :], stored.at[part])
        )
        stores[part].start()
    for store in stores:
        store.wait()


def pointwise_map(weight, cells):
    parts = 4
    in_place = pl.BlockSpec(memory_space=pltpu.HBM)
    return pl.pallas_call(
        map_kernel,
        out_shape=[
            pltpu.HBM((BLOCKS, 8, 64, 128), jnp.bfloat16),
            pltpu.HBM((BLOCKS, 64, 8, 128), jnp.bfloat16),
        ],
        in_specs=[WHOLE, in_place],
        out_specs=[in_place] * 2,
        scratch_shapes=[
            pltpu.VMEM((BLOCKS, 64, 8, 128), jnp.bfloat16),
            pltpu.VMEM((BLOCKS, 8, 64, 128), jnp.bfloat16),
            pltpu.SemaphoreType.DMA((parts,)),
            pltpu.SemaphoreType.DMA((parts,)),
        ],
        input_output_aliases={1: 1},
        cost_estimate=pl.CostEstimate(flops=270_000_000, bytes_accessed=4_000_000, transcendentals=0),
        compiler_params=pltpu.CompilerParams(vmem_limit_bytes=10 << 20),
        name="pointwise_map",
    )(weight * jnp.bfloat16(CELL_SCALE), cells)[0]


def source_block(place_ref, k, h):
    return lax.bitwise_xor(place_ref[1], h) * 8 + lax.rem(place_ref[0] + (8 - k), 8)


def mix_kernel(place_ref, *refs):
    letters, weight_ref, out_ref, coef_ref = refs[:8], refs[8], refs[9], refs[10]
    for k in range(8):
        for h in range(2):
            for part in range(2):
                for side in range(2):
                    coded = letters[k][h, part * 2 + side]
                    coef_ref[k * 2 + h, part, :, pl.ds(side * 128, 128)] = decode(coded, COEF_SCALE)
    for o in range(8):
        real = jnp.zeros((8, 256), jnp.float32)
        imag = jnp.zeros((8, 256), jnp.float32)
        for k in range(8):
            for h in range(2):
                rows = pl.ds(pl.multiple_of(source_block(place_ref, k, h) * 8, 8), 8)
                weight_real = weight_ref[0, o, rows, :]
                weight_imag = weight_ref[1, o, rows, :]
                coef_real = coef_ref[k * 2 + h, 0]
                coef_imag = coef_ref[k * 2 + h, 1]
                real += coef_real * weight_real - coef_imag * weight_imag
                imag += coef_real * weight_imag + coef_imag * weight_real
        out_ref[0, pl.ds(o, 1), :] = jnp.sum(real, 0, keepdims=True)
        out_ref[1, pl.ds(o, 1), :] = jnp.sum(imag, 0, keepdims=True)


def mix(place, letters, spec_weight):
    return pl.pallas_call(
        mix_kernel,
        out_shape=jax.ShapeDtypeStruct((2, 8, 256), jnp.float32),
        in_specs=[SCALARS] + [WHOLE] * 9,
        out_specs=WHOLE,
        scratch_shapes=[pltpu.VMEM((BLOCKS, 2, 8, 256), jnp.float32)],
        cost_estimate=pl.CostEstimate(flops=5_000_000, bytes_accessed=3_000_000, transcendentals=0),
        compiler_params=pltpu.CompilerParams(vmem_limit_bytes=8 << 20),
        name="mix",
    )(place, *letters, spec_weight)


def inverse_kernel(me_ref, bias_ref, spec_ref, depth_ref, table_x_ref, waves_y_ref, out_ref, plane_ref, line_ref, table_ref):
    row = lax.broadcasted_iota(jnp.int32, (256, 256), 0)
    lane = lax.broadcasted_iota(jnp.int32, (256, 256), 1)
    table_z = jnp.where(row // KEEP == lane % KEEP, jnp.concatenate([depth_ref[...]] * KEEP, 0), 0.0)
    real = exact_dot(spec_ref[:, 0].reshape(128, 256), table_z)
    imag = exact_dot(spec_ref[:, 1].reshape(128, 256), table_z)
    plane_real = (real[:, :128] - imag[:, 128:]).reshape(16, 8, 128)
    plane_imag = (imag[:, :128] + real[:, 128:]).reshape(16, 8, 128)
    for e in range(16):
        j = lax.bitwise_xor(me_ref[0], MIXED[e])
        plane_ref[j] = plane_real[e]
        plane_ref[16 + j] = plane_imag[e]
    for o in range(8):
        line = exact_dot(table_x_ref[...], plane_ref[:, o, :])
        line_ref[pl.ds(o * 128, 128), :] = jnp.concatenate([line[:128], line[128:]], 1)
    table_ref[...] = jnp.zeros_like(table_ref)
    for z in range(8):
        for part in range(2):
            table_ref[pl.ds(part * 128 + z * 16, 16), pl.ds(z * 128, 128)] = waves_y_ref[part]
    line_high, line_low = split(line_ref[...])
    for z in range(0, 8, 2):
        high, low = split(table_ref[:, z * 128 : (z + 2) * 128])
        field = jnp.dot(line_high, low, preferred_element_type=jnp.float32)
        field += jnp.dot(line_low, high, preferred_element_type=jnp.float32)
        field += jnp.dot(line_high, high, preferred_element_type=jnp.float32)
        for o in range(8):
            rows = slice(o * 128, (o + 1) * 128)
            out_ref[o, z] = field[rows, :128] + bias_ref[o]
            out_ref[o, z + 1] = field[rows, 128:] + bias_ref[o]


def inverse_transform(me, bias, spectrum, first_cell):
    cos_x, sin_x = plane_waves()
    table_x = jnp.asarray(
        np.concatenate([np.concatenate([cos_x.T, -sin_x.T], 1), np.concatenate([sin_x.T, cos_x.T], 1)], 0)
    )
    waves_y = jnp.asarray(np.stack([cos_x, -sin_x], 0))
    angle, row, lane = depth_angle(first_cell, (16, 256), lambda r, n: r, lambda r, n: n // 16 % 8)
    fold = jnp.where(row == 0, 1.0, 2.0) * (CELL_SCALE / GRID**3)
    depth = jnp.where(lane < 128, jnp.cos(angle), jnp.sin(angle)) * fold
    return pl.pallas_call(
        inverse_kernel,
        out_shape=pltpu.HBM((8, 8, 128, 128), jnp.float32),
        in_specs=[SCALARS] * 2 + [WHOLE] * 4,
        out_specs=WHOLE,
        scratch_shapes=[
            pltpu.VMEM((32, 8, 128), jnp.float32),
            pltpu.VMEM((1024, 256), jnp.float32),
            pltpu.VMEM((256, 1024), jnp.float32),
        ],
        cost_estimate=pl.CostEstimate(flops=2_000_000_000, bytes_accessed=5_000_000, transcendentals=0),
        compiler_params=pltpu.CompilerParams(vmem_limit_bytes=16 << 20),
        name="inverse_transform",
    )(me, bias * CELL_SCALE, spectrum, depth, table_x, waves_y)


def activate(coded, inverse):
    total = decode(coded, 1.0) + inverse
    half = total * (0.5 / CELL_SCALE)
    return (half + half * lax.erf(total * (math.sqrt(0.5) / CELL_SCALE))).astype(jnp.bfloat16)


def finish_kernel(coded_ref, inverse_ref, out_ref, kept_ref, field_ref, done_ref, fetched, stored):
    del kept_ref
    parts = fetched.shape[0]
    span = BLOCKS // parts
    fetches, stores = [], []
    for part in range(parts):
        blocks = pl.ds(part * span, span)
        fetches.append(pltpu.make_async_copy(inverse_ref.at[:, blocks], field_ref.at[:, blocks], fetched.at[part]))
        fetches[part].start()
    for part in range(parts):
        fetches[part].wait()
        for o in range(8):
            for p in range(part * span, (part + 1) * span):
                done_ref[o, p] = activate(coded_ref[p, o], field_ref[o, p])
        blocks = pl.ds(part * span, span)
        stores.append(pltpu.make_async_copy(done_ref.at[:, blocks], out_ref.at[:, blocks], stored.at[part]))
        stores[part].start()
    for store in stores:
        store.wait()


def finish(coded, inverse):
    parts = 8
    in_place = pl.BlockSpec(memory_space=pltpu.HBM)
    return pl.pallas_call(
        finish_kernel,
        out_shape=[
            pltpu.HBM((8, BLOCKS, 64, 128), jnp.bfloat16),
            pltpu.HBM((8, BLOCKS, 64, 128), jnp.float32),
        ],
        in_specs=[WHOLE, in_place],
        out_specs=[in_place] * 2,
        scratch_shapes=[
            pltpu.VMEM((8, BLOCKS, 64, 128), jnp.float32),
            pltpu.VMEM((8, BLOCKS, 64, 128), jnp.bfloat16),
            pltpu.SemaphoreType.DMA((parts,)),
            pltpu.SemaphoreType.DMA((parts,)),
        ],
        input_output_aliases={1: 1},
        cost_estimate=pl.CostEstimate(flops=30_000_000, bytes_accessed=8_000_000, transcendentals=0),
        compiler_params=pltpu.CompilerParams(vmem_limit_bytes=12 << 20),
        name="finish",
    )(coded, inverse)[0]


def on_device(field, local_weight, bias, spec_weight):
    slab, chan = lax.axis_index("slab"), lax.axis_index("chan")
    first_cell = slab * 8
    x_hi = chan // 8
    place = jnp.stack([chan % 8, x_hi]).astype(jnp.int32)
    planes = field[0]
    blocks = planes.reshape(8, BLOCKS, 64, 128)
    cells = lax.all_to_all(cut(blocks), "chan", 0, 0, tiled=True)
    partial = forward_transform(planes, first_cell)
    owned = slab_sum(partial)
    own_coef = encode(owned, COEF_SCALE).reshape(2, 8, 2, 128).transpose(0, 2, 1, 3).reshape(4, 8, 128)
    other_coef = lax.ppermute(own_coef, "chan", chan_perm(1, 0))
    letter = jnp.stack([own_coef, other_coef], 0)
    letters = [letter] + [lax.ppermute(letter, "chan", chan_perm(0, k)) for k in range(1, 8)]
    coded = pointwise_map(local_weight, cells)
    coded = lax.all_to_all(coded, "chan", 0, 0, tiled=True)
    mixed = mix(place, letters, spec_weight)
    spectrum = slab_gather(mixed)
    me = jnp.reshape(slab, (1,)).astype(jnp.int32)
    offset = lax.dynamic_slice_in_dim(bias, chan * 8, 8, 0)
    inverse = inverse_transform(me, offset, spectrum, first_cell).reshape(8, BLOCKS, 64, 128)
    done = finish(coded, inverse)
    return done.reshape(1, 8, 8, 128, 128)


def solution(mesh):
    placed = (P(None, "chan", "slab", None, None), P(), P(), P(None, "chan", None, "slab"))
    return jax.shard_map(
        on_device,
        mesh=mesh,
        in_specs=placed,
        out_specs=P(None, "chan", "slab", None, None),
        check_vma=False,
    )
```

```python
import math

import jax
import jax.numpy as jnp
import numpy as np
from jax import lax
from jax.experimental import pallas as pl
from jax.experimental.pallas import tpu as pltpu
from jax.sharding import PartitionSpec as P


GRID = 128
KEEP = 16
BLOCKS = 16
LATE = 16
EARLY = 64 - LATE
PRECISE = lax.Precision.HIGHEST
CELL_SCALE = 2.0**20
COEF_SCALE = 2.0**6
WHOLE = pl.BlockSpec(memory_space=pltpu.VMEM)
SCALARS = pl.BlockSpec(memory_space=pltpu.SMEM)


def waves(freqs, positions):
    angle = 2.0 * math.pi * (freqs * positions % GRID).astype(np.float32) / np.float32(GRID)
    return np.cos(angle).astype(np.float32), np.sin(angle).astype(np.float32)


def plane_waves():
    index = np.arange(KEEP)
    freqs = np.where(index < KEEP // 2, index, index + GRID - KEEP)
    return waves(freqs[:, None], np.arange(GRID)[None, :])


def depth_angle(first_cell, shape, mode, cell):
    row = lax.broadcasted_iota(jnp.int32, shape, 0)
    lane = lax.broadcasted_iota(jnp.int32, shape, 1)
    turns = mode(row, lane) * (first_cell + cell(row, lane)) % GRID
    return 2.0 * math.pi * turns.astype(jnp.float32) / GRID, row, lane


def exact_dot(left, right):
    return jnp.dot(left, right, precision=PRECISE, preferred_element_type=jnp.float32)


def split(value):
    high = value.astype(jnp.bfloat16)
    return high, (value - high.astype(jnp.float32)).astype(jnp.bfloat16)


def encode(value, scale):
    value = value * scale
    return (value * jnp.abs(value) * (value * value)).astype(jnp.bfloat16)


def decode(coded, scale):
    coded = coded.astype(jnp.float32)
    size = lax.rsqrt(lax.rsqrt(jnp.abs(coded)))
    if scale != 1.0:
        size = size * (1.0 / scale)
    return jnp.where(coded < 0, -size, size)


def slab_perm(dx, dy, dc):
    pairs = []
    for a in range(2):
        for b in range(4):
            for c in range(2):
                pairs.append(((a * 4 + b) * 2 + c, ((a ^ dx) * 4 + (b ^ dy)) * 2 + (c ^ dc)))
    return pairs


def chan_perm(dx, dz):
    return [(h * 8 + z, (h ^ dx) * 8 + (z + dz) % 8) for h in range(2) for z in range(8)]


def halve(value, axis, bit, perm):
    own = lax.dynamic_index_in_dim(value, bit, axis, keepdims=False)
    other = lax.dynamic_index_in_dim(value, 1 - bit, axis, keepdims=False)
    return own + lax.ppermute(other, "slab", perm)


def slab_sum(partial):
    me = lax.axis_index("slab")
    value = partial.reshape(2, 2, 2, 2, *partial.shape[1:])
    value = halve(value, 3, me % 2, slab_perm(0, 0, 1))
    value = halve(value, 1, me // 4 % 2, slab_perm(0, 2, 0))
    value = halve(value, 1, me // 2 % 2, slab_perm(0, 1, 0))
    return halve(value, 0, me // 8, slab_perm(1, 0, 0))


def slab_gather(value):
    value = value[None]
    for step in ((1, 0, 0), (0, 1, 0), (0, 2, 0), (0, 0, 1)):
        other = lax.ppermute(value, "slab", slab_perm(*step))
        value = jnp.concatenate([value, other], 0)
    return value


MIXED = tuple((e & 1) * 8 | (e >> 1 & 1) * 2 | (e >> 2 & 1) * 4 | e >> 3 for e in range(16))


def forward_kernel(field_ref, table_x_ref, table_y_ref, depth_ref, out_ref, wave_ref, table_z_ref):
    table_y = table_y_ref[...]
    lane = lax.broadcasted_iota(jnp.int32, (KEEP, 512), 1)
    row = lax.broadcasted_iota(jnp.int32, (KEEP, 512), 0)
    same_mode = lane // KEEP % KEEP == row
    for z in range(8):
        sections = []
        for c in range(8):
            section = jnp.dot(table_x_ref[...], field_ref[c, z], preferred_element_type=jnp.float32)
            sections.append(jnp.concatenate([section[:KEEP], section[KEEP:]], 1))
        wave_ref[:, pl.ds(z * 32, 32)] = exact_dot(jnp.concatenate(sections, 0), table_y)
        for part in range(2):
            rows = pl.ds(z * 32 + part * KEEP, KEEP)
            depth = jnp.broadcast_to(depth_ref[pl.ds(z * 2 + part, 1), :], (KEEP, 512))
            table_z_ref[rows, :] = jnp.where(same_mode, depth, 0.0)
    coefs = exact_dot(wave_ref[...], table_z_ref[...]).reshape(8, KEEP, 512).transpose(1, 0, 2)
    out_ref[:, 0] = coefs[:, :, :256]
    out_ref[:, 1] = coefs[:, :, 256:]


def forward_transform(field, first_cell):
    cos_x, sin_x = plane_waves()
    table_x = jnp.asarray(np.concatenate([cos_x, -sin_x], 0)).astype(jnp.bfloat16)
    table_y = jnp.asarray(
        np.concatenate([np.concatenate([cos_x.T, -sin_x.T], 1), np.concatenate([sin_x.T, cos_x.T], 1)], 0)
    )
    angle, row, lane = depth_angle(first_cell, (16, 512), lambda r, n: n % 16, lambda r, n: r // 2)
    from_part, to_part = row % 2, lane // 256
    turned = jnp.where(from_part == 1, jnp.sin(angle), -jnp.sin(angle))
    depth = jnp.where(from_part == to_part, jnp.cos(angle), turned)
    return pl.pallas_call(
        forward_kernel,
        out_shape=jax.ShapeDtypeStruct((KEEP, 2, 8, 256), jnp.float32),
        in_specs=[WHOLE] * 4,
        out_specs=WHOLE,
        scratch_shapes=[pltpu.VMEM((128, 256), jnp.float32), pltpu.VMEM((256, 512), jnp.float32)],
        cost_estimate=pl.CostEstimate(flops=200_000_000, bytes_accessed=3_000_000, transcendentals=0),
        compiler_params=pltpu.CompilerParams(vmem_limit_bytes=12 << 20),
        name="forward_transform",
    )(field, table_x, table_y, depth)


def cut_kernel(field_ref, early_ref, own_ref, other_ref, block_ref, turned_ref, late_ref, fetched, stored):
    x_hi = lax.shift_right_logical(lax.axis_index("chan"), 3)
    parts = fetched.shape[0]
    span = BLOCKS // parts
    fetches, stores = [], []
    for part in range(parts):
        blocks = pl.ds(part * span, span)
        fetches.append(pltpu.make_async_copy(field_ref.at[:, blocks], block_ref.at[:, blocks], fetched.at[part]))
        fetches[part].start()
    for part in range(parts):
        fetches[part].wait()
        for p in range(part * span, (part + 1) * span):
            block = block_ref[:, p].astype(jnp.float32)
            turned = block.transpose(1, 0, 2).astype(jnp.bfloat16)
            turned_ref[p] = turned[:EARLY]
            late_ref[lax.bitwise_xor(x_hi, p // 8), p % 8] = turned[EARLY:]
        blocks = pl.ds(part * span, span)
        stores.append(pltpu.make_async_copy(turned_ref.at[blocks], early_ref.at[blocks], stored.at[part]))
        stores[part].start()
    own_ref[...] = late_ref[0]
    other_ref[...] = late_ref[1]
    for store in stores:
        store.wait()


def cut(blocks):
    parts = 8
    in_place = pl.BlockSpec(memory_space=pltpu.HBM)
    return pl.pallas_call(
        cut_kernel,
        out_shape=[pltpu.HBM((BLOCKS, EARLY, 8, 128), jnp.bfloat16)]
        + [jax.ShapeDtypeStruct((8, LATE, 8, 128), jnp.bfloat16)] * 2,
        in_specs=[in_place],
        out_specs=[in_place, WHOLE, WHOLE],
        scratch_shapes=[
            pltpu.VMEM((8, BLOCKS, 64, 128), jnp.bfloat16),
            pltpu.VMEM((BLOCKS, EARLY, 8, 128), jnp.bfloat16),
            pltpu.VMEM((2, 8, LATE, 8, 128), jnp.bfloat16),
            pltpu.SemaphoreType.DMA((parts,)),
            pltpu.SemaphoreType.DMA((parts,)),
        ],
        cost_estimate=pl.CostEstimate(flops=1_000_000, bytes_accessed=4_000_000, transcendentals=0),
        compiler_params=pltpu.CompilerParams(vmem_limit_bytes=60 << 20),
        name="cut",
    )(blocks)


def map_rows(weight_ref, cells_ref, first):
    coded = []
    for x in range(first, first + 8, 2):
        pair = [cells_ref[:, x + near].reshape(128, 128) for near in range(2)]
        mapped = jnp.dot(weight_ref[...], jnp.concatenate(pair, 1), preferred_element_type=jnp.float32)
        mapped = mapped * jnp.abs(mapped) * (mapped * mapped)
        coded += [mapped[:, :128], mapped[:, 128:]]
    turned = jnp.stack(coded, 0).transpose(1, 0, 2)
    return turned.reshape(BLOCKS, 8, 8, 128).astype(jnp.bfloat16)


def map_kernel(weight_ref, cells_ref, out_ref, kept_ref, block_ref, held_ref, fetched, stored):
    del kept_ref
    fetches, stores = [], []
    spans = [(0, EARLY % 16)] * (EARLY % 16 > 0) + [(first, 16) for first in range(EARLY % 16, EARLY, 16)]
    for part, (first, rows) in enumerate(spans):
        span = pl.ds(first, rows)
        fetches.append(pltpu.make_async_copy(cells_ref.at[:, span], block_ref.at[:, span], fetched.at[part]))
        fetches[part].start()
    for part, (start, rows) in enumerate(spans):
        fetches[part].wait()
        for first in range(start, start + rows, 8):
            held_ref[:, :, pl.ds(first, 8), :] = map_rows(weight_ref, block_ref, first)
        span = pl.ds(start, rows)
        stores.append(
            pltpu.make_async_copy(held_ref.at[:, :, span, :], out_ref.at[:, :, span, :], stored.at[part])
        )
        stores[part].start()
    for store in stores:
        store.wait()


def map_early(weight, cells):
    in_place = pl.BlockSpec(memory_space=pltpu.HBM)
    return pl.pallas_call(
        map_kernel,
        out_shape=[
            pltpu.HBM((BLOCKS, 8, EARLY, 128), jnp.bfloat16),
            pltpu.HBM((BLOCKS, EARLY, 8, 128), jnp.bfloat16),
        ],
        in_specs=[WHOLE, in_place],
        out_specs=[in_place] * 2,
        scratch_shapes=[
            pltpu.VMEM((BLOCKS, EARLY, 8, 128), jnp.bfloat16),
            pltpu.VMEM((BLOCKS, 8, EARLY, 128), jnp.bfloat16),
            pltpu.SemaphoreType.DMA((4,)),
            pltpu.SemaphoreType.DMA((4,)),
        ],
        input_output_aliases={1: 1},
        cost_estimate=pl.CostEstimate(flops=270_000_000, bytes_accessed=4_000_000, transcendentals=0),
        compiler_params=pltpu.CompilerParams(vmem_limit_bytes=10 << 20),
        name="map_early",
    )(weight, cells)[0]


def source_block(place_ref, k, h):
    return lax.bitwise_xor(place_ref[1], h) * 8 + lax.rem(place_ref[0] + (8 - k), 8)


def pack_kernel(place_ref, own_cells_ref, other_cells_ref, own_coef_ref, other_coef_ref, *letters):
    for k in range(8):
        target = lax.rem(place_ref[0] + k, 8)
        for h, (cells_ref, coef_ref) in enumerate(
            ((own_cells_ref, own_coef_ref), (other_cells_ref, other_coef_ref))
        ):
            letters[k][h, :LATE] = cells_ref[target]
            letters[k][h, LATE:] = coef_ref[...]


def pack(place, own_cells, other_cells, own_coef, other_coef):
    return pl.pallas_call(
        pack_kernel,
        out_shape=[jax.ShapeDtypeStruct((2, LATE + 4, 8, 128), jnp.bfloat16)] * 8,
        in_specs=[SCALARS] + [WHOLE] * 4,
        out_specs=[WHOLE] * 8,
        cost_estimate=pl.CostEstimate(flops=0, bytes_accessed=800_000, transcendentals=0),
        compiler_params=pltpu.CompilerParams(vmem_limit_bytes=4 << 20),
        name="pack",
    )(place, own_cells, other_cells, own_coef, other_coef)


def map_late_kernel(place_ref, weight_ref, *refs):
    letters, own_ref, other_ref, cells_ref, held_ref = refs[:8], refs[8], refs[9], refs[10], refs[11]
    for k in range(8):
        for h in range(2):
            cells_ref[source_block(place_ref, k, h)] = letters[k][h, :LATE]
    for first in range(0, LATE, 8):
        held_ref[:, :, pl.ds(first, 8), :] = map_rows(weight_ref, cells_ref, first)
    own_ref[...] = held_ref[pl.ds(place_ref[1] * 8, 8)]
    other_ref[...] = held_ref[pl.ds(8 - place_ref[1] * 8, 8)]


def map_late(place, weight, letters):
    return pl.pallas_call(
        map_late_kernel,
        out_shape=[jax.ShapeDtypeStruct((8, 8, LATE, 128), jnp.bfloat16)] * 2,
        in_specs=[SCALARS] + [WHOLE] * 9,
        out_specs=[WHOLE] * 2,
        scratch_shapes=[
            pltpu.VMEM((BLOCKS, LATE, 8, 128), jnp.bfloat16),
            pltpu.VMEM((BLOCKS, 8, LATE, 128), jnp.bfloat16),
        ],
        cost_estimate=pl.CostEstimate(flops=40_000_000, bytes_accessed=600_000, transcendentals=0),
        compiler_params=pltpu.CompilerParams(vmem_limit_bytes=6 << 20),
        name="map_late",
    )(place, weight, *letters)


def sort_kernel(place_ref, own_ref, other_ref, *letters):
    for k in range(8):
        target = lax.rem(place_ref[0] + k, 8)
        letters[k][0] = own_ref[target]
        letters[k][1] = other_ref[target]


def sort(place, own, other):
    return pl.pallas_call(
        sort_kernel,
        out_shape=[jax.ShapeDtypeStruct((2, 8, LATE, 128), jnp.bfloat16)] * 8,
        in_specs=[SCALARS] + [WHOLE] * 2,
        out_specs=[WHOLE] * 8,
        cost_estimate=pl.CostEstimate(flops=0, bytes_accessed=600_000, transcendentals=0),
        compiler_params=pltpu.CompilerParams(vmem_limit_bytes=4 << 20),
        name="sort",
    )(place, own, other)


def mix_kernel(place_ref, *refs):
    letters, weight_ref, out_ref, coef_ref = refs[:8], refs[8], refs[9], refs[10]
    for k in range(8):
        for h in range(2):
            for part in range(2):
                for side in range(2):
                    coded = letters[k][h, LATE + part * 2 + side]
                    coef_ref[k * 2 + h, part, :, pl.ds(side * 128, 128)] = decode(coded, COEF_SCALE)
    for o in range(8):
        real = jnp.zeros((8, 256), jnp.float32)
        imag = jnp.zeros((8, 256), jnp.float32)
        for k in range(8):
            for h in range(2):
                rows = pl.ds(pl.multiple_of(source_block(place_ref, k, h) * 8, 8), 8)
                weight_real = weight_ref[0, o, rows, :]
                weight_imag = weight_ref[1, o, rows, :]
                coef_real = coef_ref[k * 2 + h, 0]
                coef_imag = coef_ref[k * 2 + h, 1]
                real += coef_real * weight_real - coef_imag * weight_imag
                imag += coef_real * weight_imag + coef_imag * weight_real
        out_ref[0, pl.ds(o, 1), :] = jnp.sum(real, 0, keepdims=True)
        out_ref[1, pl.ds(o, 1), :] = jnp.sum(imag, 0, keepdims=True)


def mix(place, letters, spec_weight):
    return pl.pallas_call(
        mix_kernel,
        out_shape=jax.ShapeDtypeStruct((2, 8, 256), jnp.float32),
        in_specs=[SCALARS] + [WHOLE] * 9,
        out_specs=WHOLE,
        scratch_shapes=[pltpu.VMEM((BLOCKS, 2, 8, 256), jnp.float32)],
        cost_estimate=pl.CostEstimate(flops=5_000_000, bytes_accessed=3_000_000, transcendentals=0),
        compiler_params=pltpu.CompilerParams(vmem_limit_bytes=8 << 20),
        name="mix",
    )(place, *letters, spec_weight)


def inverse_kernel(me_ref, bias_ref, spec_ref, depth_ref, table_x_ref, waves_y_ref, out_ref, late_ref, *scratch):
    plane_ref, line_ref, table_ref, held_ref, stored = scratch
    row = lax.broadcasted_iota(jnp.int32, (256, 256), 0)
    lane = lax.broadcasted_iota(jnp.int32, (256, 256), 1)
    table_z = jnp.where(row // KEEP == lane % KEEP, jnp.concatenate([depth_ref[...]] * KEEP, 0), 0.0)
    real = exact_dot(spec_ref[:, 0].reshape(128, 256), table_z)
    imag = exact_dot(spec_ref[:, 1].reshape(128, 256), table_z)
    plane_real = (real[:, :128] - imag[:, 128:]).reshape(16, 8, 128)
    plane_imag = (imag[:, :128] + real[:, 128:]).reshape(16, 8, 128)
    for e in range(16):
        j = lax.bitwise_xor(me_ref[0], MIXED[e])
        plane_ref[j] = plane_real[e]
        plane_ref[16 + j] = plane_imag[e]
    for o in range(8):
        line = exact_dot(table_x_ref[...], plane_ref[:, o, :])
        line_ref[pl.ds(o * 128, 128), :] = jnp.concatenate([line[:128], line[128:]], 1)
    table_ref[...] = jnp.zeros_like(table_ref)
    for z in range(8):
        for part in range(2):
            table_ref[pl.ds(part * 128 + z * 16, 16), pl.ds(z * 128, 128)] = waves_y_ref[part]
    line_high, line_low = split(line_ref[...])
    stores = []
    for z in range(0, 8, 2):
        high, low = split(table_ref[:, z * 128 : (z + 2) * 128])
        field = jnp.dot(line_high, low, preferred_element_type=jnp.float32)
        field += jnp.dot(line_low, high, preferred_element_type=jnp.float32)
        field += jnp.dot(line_high, high, preferred_element_type=jnp.float32)
        for o in range(8):
            rows = slice(o * 128, (o + 1) * 128)
            for near in range(2):
                plane = field[rows, near * 128 : (near + 1) * 128] + bias_ref[o]
                for half in range(2):
                    block = (z + near) * 2 + half
                    held_ref[o, block] = plane[half * 64 : half * 64 + EARLY]
                    late_ref[o, block] = plane[half * 64 + EARLY : (half + 1) * 64]
        blocks = pl.ds(z * 2, 4)
        stores.append(pltpu.make_async_copy(held_ref.at[:, blocks], out_ref.at[:, blocks], stored.at[z // 2]))
        stores[z // 2].start()
    for store in stores:
        store.wait()


def inverse_transform(me, bias, spectrum, first_cell):
    cos_x, sin_x = plane_waves()
    table_x = jnp.asarray(
        np.concatenate([np.concatenate([cos_x.T, -sin_x.T], 1), np.concatenate([sin_x.T, cos_x.T], 1)], 0)
    )
    waves_y = jnp.asarray(np.stack([cos_x, -sin_x], 0))
    angle, row, lane = depth_angle(first_cell, (16, 256), lambda r, n: r, lambda r, n: n // 16 % 8)
    fold = jnp.where(row == 0, 1.0, 2.0) * (CELL_SCALE / GRID**3)
    depth = jnp.where(lane < 128, jnp.cos(angle), jnp.sin(angle)) * fold
    return pl.pallas_call(
        inverse_kernel,
        out_shape=[
            pltpu.HBM((8, BLOCKS, EARLY, 128), jnp.float32),
            jax.ShapeDtypeStruct((8, BLOCKS, LATE, 128), jnp.float32),
        ],
        in_specs=[SCALARS] * 2 + [WHOLE] * 4,
        out_specs=[pl.BlockSpec(memory_space=pltpu.HBM), WHOLE],
        scratch_shapes=[
            pltpu.VMEM((32, 8, 128), jnp.float32),
            pltpu.VMEM((1024, 256), jnp.float32),
            pltpu.VMEM((256, 1024), jnp.float32),
            pltpu.VMEM((8, BLOCKS, EARLY, 128), jnp.float32),
            pltpu.SemaphoreType.DMA((4,)),
        ],
        cost_estimate=pl.CostEstimate(flops=2_000_000_000, bytes_accessed=5_000_000, transcendentals=0),
        compiler_params=pltpu.CompilerParams(vmem_limit_bytes=16 << 20),
        name="inverse_transform",
    )(me, bias * CELL_SCALE, spectrum, depth, table_x, waves_y)


def activate(coded, inverse):
    total = decode(coded, 1.0) + inverse
    half = total * (0.5 / CELL_SCALE)
    return (half + half * lax.erf(total * (math.sqrt(0.5) / CELL_SCALE))).astype(jnp.bfloat16)


def finish_early_kernel(coded_ref, inverse_ref, out_ref, kept_ref, field_ref, done_ref, fetched, stored):
    del kept_ref
    parts = fetched.shape[0]
    span = BLOCKS // parts
    fetches, stores = [], []
    for part in range(parts):
        blocks = pl.ds(part * span, span)
        fetches.append(pltpu.make_async_copy(inverse_ref.at[:, blocks], field_ref.at[:, blocks], fetched.at[part]))
        fetches[part].start()
    for part in range(parts):
        fetches[part].wait()
        for o in range(8):
            for p in range(part * span, (part + 1) * span):
                done_ref[o, p] = activate(coded_ref[p, o], field_ref[o, p])
        blocks = pl.ds(part * span, span)
        target = out_ref.at[:, blocks, pl.ds(0, EARLY), :]
        stores.append(pltpu.make_async_copy(done_ref.at[:, blocks], target, stored.at[part]))
        stores[part].start()
    for store in stores:
        store.wait()


def finish_early(coded, inverse):
    parts = 8
    in_place = pl.BlockSpec(memory_space=pltpu.HBM)
    return pl.pallas_call(
        finish_early_kernel,
        out_shape=[
            pltpu.HBM((8, BLOCKS, 64, 128), jnp.bfloat16),
            pltpu.HBM((8, BLOCKS, EARLY, 128), jnp.float32),
        ],
        in_specs=[WHOLE, in_place],
        out_specs=[in_place] * 2,
        scratch_shapes=[
            pltpu.VMEM((8, BLOCKS, EARLY, 128), jnp.float32),
            pltpu.VMEM((8, BLOCKS, EARLY, 128), jnp.bfloat16),
            pltpu.SemaphoreType.DMA((parts,)),
            pltpu.SemaphoreType.DMA((parts,)),
        ],
        input_output_aliases={1: 1},
        cost_estimate=pl.CostEstimate(flops=30_000_000, bytes_accessed=8_000_000, transcendentals=0),
        compiler_params=pltpu.CompilerParams(vmem_limit_bytes=12 << 20),
        name="finish_early",
    )(coded, inverse)[0]


def finish_late_kernel(place_ref, inverse_ref, *refs):
    letters, out_ref, done_ref, stored = refs[:8], refs[9], refs[10], refs[11]
    for k in range(8):
        for h in range(2):
            block = source_block(place_ref, k, h)
            for o in range(8):
                done_ref[o, block] = activate(letters[k][h, o], inverse_ref[o, block])
    store = pltpu.make_async_copy(done_ref, out_ref.at[:, :, pl.ds(EARLY, LATE), :], stored)
    store.start()
    store.wait()


def finish_late(place, inverse, letters, partial):
    in_place = pl.BlockSpec(memory_space=pltpu.HBM)
    return pl.pallas_call(
        finish_late_kernel,
        out_shape=pltpu.HBM((8, BLOCKS, 64, 128), jnp.bfloat16),
        in_specs=[SCALARS] + [WHOLE] * 9 + [in_place],
        out_specs=in_place,
        scratch_shapes=[pltpu.VMEM((8, BLOCKS, LATE, 128), jnp.bfloat16), pltpu.SemaphoreType.DMA],
        input_output_aliases={10: 0},
        cost_estimate=pl.CostEstimate(flops=4_000_000, bytes_accessed=1_200_000, transcendentals=0),
        compiler_params=pltpu.CompilerParams(vmem_limit_bytes=6 << 20),
        name="finish_late",
    )(place, inverse, *letters, partial)


def z_letters(letters):
    arrived = [letters[0]]
    for k in range(1, 8):
        arrived.append(lax.ppermute(letters[k], "chan", chan_perm(0, k)))
    return arrived


def on_device(field, local_weight, bias, spec_weight):
    slab, chan = lax.axis_index("slab"), lax.axis_index("chan")
    first_cell = slab * 8
    x_hi = chan // 8
    place = jnp.stack([chan % 8, x_hi]).astype(jnp.int32)
    planes = field[0]
    blocks = planes.reshape(8, BLOCKS, 64, 128)
    weight = local_weight * jnp.bfloat16(CELL_SCALE)
    cells, own_cells, other_cells = cut(blocks)
    cells = lax.all_to_all(cells, "chan", 0, 0, tiled=True)
    other_cells = lax.ppermute(other_cells, "chan", chan_perm(1, 0))
    partial = forward_transform(planes, first_cell)
    owned = slab_sum(partial)
    own_coef = encode(owned, COEF_SCALE).reshape(2, 8, 2, 128).transpose(0, 2, 1, 3).reshape(4, 8, 128)
    other_coef = lax.ppermute(own_coef, "chan", chan_perm(1, 0))
    letters = pack(place, own_cells, other_cells, own_coef, other_coef)
    letters = z_letters(letters)
    coded = map_early(weight, cells)
    coded = lax.all_to_all(coded, "chan", 0, 0, tiled=True)
    mixed = mix(place, letters, spec_weight)
    own_late, other_late = map_late(place, weight, letters)
    other_late = lax.ppermute(other_late, "chan", chan_perm(1, 0))
    answers = sort(place, own_late, other_late)
    answers = z_letters(answers)
    spectrum = slab_gather(mixed)
    me = jnp.reshape(slab, (1,)).astype(jnp.int32)
    offset = lax.dynamic_slice_in_dim(bias, chan * 8, 8, 0)
    inverse, inverse_late = inverse_transform(me, offset, spectrum, first_cell)
    done = finish_early(coded, inverse)
    done = finish_late(place, inverse_late, answers, done)
    return done.reshape(1, 8, 8, 128, 128)


def solution(mesh):
    placed = (P(None, "chan", "slab", None, None), P(), P(), P(None, "chan", None, "slab"))
    return jax.shard_map(
        on_device,
        mesh=mesh,
        in_specs=placed,
        out_specs=P(None, "chan", "slab", None, None),
        check_vma=False,
    )
```

```python
import math

import jax
import jax.numpy as jnp
import numpy as np
from jax import lax
from jax.experimental import pallas as pl
from jax.experimental.pallas import tpu as pltpu
from jax.sharding import PartitionSpec as P


GRID = 128
KEEP = 16
BLOCKS = 16
LATE = 16
EARLY = 64 - LATE
PRECISE = lax.Precision.HIGHEST
CELL_SCALE = 2.0**20
COEF_SCALE = 2.0**6
WHOLE = pl.BlockSpec(memory_space=pltpu.VMEM)
SCALARS = pl.BlockSpec(memory_space=pltpu.SMEM)


def waves(freqs, positions):
    angle = 2.0 * math.pi * (freqs * positions % GRID).astype(np.float32) / np.float32(GRID)
    return np.cos(angle).astype(np.float32), np.sin(angle).astype(np.float32)


def plane_waves():
    index = np.arange(KEEP)
    freqs = np.where(index < KEEP // 2, index, index + GRID - KEEP)
    return waves(freqs[:, None], np.arange(GRID)[None, :])


def depth_angle(first_cell, shape, mode, cell):
    row = lax.broadcasted_iota(jnp.int32, shape, 0)
    lane = lax.broadcasted_iota(jnp.int32, shape, 1)
    turns = mode(row, lane) * (first_cell + cell(row, lane)) % GRID
    return 2.0 * math.pi * turns.astype(jnp.float32) / GRID, row, lane


def exact_dot(left, right):
    return jnp.dot(left, right, precision=PRECISE, preferred_element_type=jnp.float32)


def split(value):
    high = value.astype(jnp.bfloat16)
    return high, (value - high.astype(jnp.float32)).astype(jnp.bfloat16)


def encode(value, scale):
    value = value * scale
    return (value * jnp.abs(value) * (value * value)).astype(jnp.bfloat16)


def decode(coded, scale):
    coded = coded.astype(jnp.float32)
    size = lax.rsqrt(lax.rsqrt(jnp.abs(coded)))
    if scale != 1.0:
        size = size * (1.0 / scale)
    return jnp.where(coded < 0, -size, size)


def slab_perm(dx, dy, dc):
    pairs = []
    for a in range(2):
        for b in range(4):
            for c in range(2):
                pairs.append(((a * 4 + b) * 2 + c, ((a ^ dx) * 4 + (b ^ dy)) * 2 + (c ^ dc)))
    return pairs


def chan_perm(dx, dz):
    return [(h * 8 + z, (h ^ dx) * 8 + (z + dz) % 8) for h in range(2) for z in range(8)]


def halve(value, axis, bit, perm):
    own = lax.dynamic_index_in_dim(value, bit, axis, keepdims=False)
    other = lax.dynamic_index_in_dim(value, 1 - bit, axis, keepdims=False)
    return own + lax.ppermute(other, "slab", perm)


def slab_sum(partial):
    me = lax.axis_index("slab")
    value = partial.reshape(2, 2, 2, 2, *partial.shape[1:])
    value = halve(value, 3, me % 2, slab_perm(0, 0, 1))
    value = halve(value, 1, me // 4 % 2, slab_perm(0, 2, 0))
    value = halve(value, 1, me // 2 % 2, slab_perm(0, 1, 0))
    return halve(value, 0, me // 8, slab_perm(1, 0, 0))


def slab_gather(value):
    value = value[None]
    for step in ((1, 0, 0), (0, 1, 0), (0, 2, 0), (0, 0, 1)):
        other = lax.ppermute(value, "slab", slab_perm(*step))
        value = jnp.concatenate([value, other], 0)
    return value


MIXED = tuple((e & 1) * 8 | (e >> 1 & 1) * 2 | (e >> 2 & 1) * 4 | e >> 3 for e in range(16))


def forward_kernel(field_ref, table_x_ref, table_y_ref, depth_ref, out_ref, wave_ref, table_z_ref):
    table_y = table_y_ref[...]
    lane = lax.broadcasted_iota(jnp.int32, (KEEP, 512), 1)
    row = lax.broadcasted_iota(jnp.int32, (KEEP, 512), 0)
    same_mode = lane // KEEP % KEEP == row
    for z in range(8):
        sections = []
        for c in range(8):
            section = jnp.dot(table_x_ref[...], field_ref[c, z], preferred_element_type=jnp.float32)
            sections.append(jnp.concatenate([section[:KEEP], section[KEEP:]], 1))
        wave_ref[:, pl.ds(z * 32, 32)] = exact_dot(jnp.concatenate(sections, 0), table_y)
        for part in range(2):
            rows = pl.ds(z * 32 + part * KEEP, KEEP)
            depth = jnp.broadcast_to(depth_ref[pl.ds(z * 2 + part, 1), :], (KEEP, 512))
            table_z_ref[rows, :] = jnp.where(same_mode, depth, 0.0)
    coefs = exact_dot(wave_ref[...], table_z_ref[...]).reshape(8, KEEP, 512).transpose(1, 0, 2)
    out_ref[:, 0] = coefs[:, :, :256]
    out_ref[:, 1] = coefs[:, :, 256:]


def forward_transform(field, first_cell):
    cos_x, sin_x = plane_waves()
    table_x = jnp.asarray(np.concatenate([cos_x, -sin_x], 0)).astype(jnp.bfloat16)
    table_y = jnp.asarray(
        np.concatenate([np.concatenate([cos_x.T, -sin_x.T], 1), np.concatenate([sin_x.T, cos_x.T], 1)], 0)
    )
    angle, row, lane = depth_angle(first_cell, (16, 512), lambda r, n: n % 16, lambda r, n: r // 2)
    from_part, to_part = row % 2, lane // 256
    turned = jnp.where(from_part == 1, jnp.sin(angle), -jnp.sin(angle))
    depth = jnp.where(from_part == to_part, jnp.cos(angle), turned)
    return pl.pallas_call(
        forward_kernel,
        out_shape=jax.ShapeDtypeStruct((KEEP, 2, 8, 256), jnp.float32),
        in_specs=[WHOLE] * 4,
        out_specs=WHOLE,
        scratch_shapes=[pltpu.VMEM((128, 256), jnp.float32), pltpu.VMEM((256, 512), jnp.float32)],
        cost_estimate=pl.CostEstimate(flops=200_000_000, bytes_accessed=3_000_000, transcendentals=0),
        compiler_params=pltpu.CompilerParams(vmem_limit_bytes=12 << 20),
        name="forward_transform",
    )(field, table_x, table_y, depth)


def cut_kernel(field_ref, early_ref, own_ref, other_ref, block_ref, turned_ref, late_ref, fetched, stored, parted):
    x_hi = lax.shift_right_logical(lax.axis_index("chan"), 3)
    parts = fetched.shape[0]
    span = BLOCKS // parts
    fetches, stores = [], []
    for part in range(parts):
        blocks = pl.ds(part * span, span)
        fetches.append(pltpu.make_async_copy(field_ref.at[:, blocks], block_ref.at[:, blocks], fetched.at[part]))
        fetches[part].start()
    for part in range(parts):
        fetches[part].wait()
        for p in range(part * span, (part + 1) * span):
            block = block_ref[:, p].astype(jnp.float32)
            turned = block.transpose(1, 0, 2).astype(jnp.bfloat16)
            turned_ref[p] = turned[:EARLY]
            late_ref[p // 8, p % 8] = turned[EARLY:]
        blocks = pl.ds(part * span, span)
        stores.append(pltpu.make_async_copy(turned_ref.at[blocks], early_ref.at[blocks], stored.at[part]))
        stores[part].start()
        if (part + 1) % (parts // 2) == 0:
            half = part // (parts // 2)
            for target, side in ((own_ref, half), (other_ref, 1 - half)):

                @pl.when(x_hi == side)
                def _():
                    pltpu.make_async_copy(late_ref.at[half], target, parted.at[half]).start()

    for half in range(2):
        stores.append(pltpu.make_async_copy(late_ref.at[half], own_ref, parted.at[half]))
    for store in stores:
        store.wait()


def cut(blocks):
    parts = 8
    in_place = pl.BlockSpec(memory_space=pltpu.HBM)
    return pl.pallas_call(
        cut_kernel,
        out_shape=[pltpu.HBM((BLOCKS, EARLY, 8, 128), jnp.bfloat16)]
        + [pltpu.HBM((8, LATE, 8, 128), jnp.bfloat16)] * 2,
        in_specs=[in_place],
        out_specs=[in_place] * 3,
        scratch_shapes=[
            pltpu.VMEM((8, BLOCKS, 64, 128), jnp.bfloat16),
            pltpu.VMEM((BLOCKS, EARLY, 8, 128), jnp.bfloat16),
            pltpu.VMEM((2, 8, LATE, 8, 128), jnp.bfloat16),
            pltpu.SemaphoreType.DMA((parts,)),
            pltpu.SemaphoreType.DMA((parts,)),
            pltpu.SemaphoreType.DMA((2,)),
        ],
        cost_estimate=pl.CostEstimate(flops=1_000_000, bytes_accessed=4_000_000, transcendentals=0),
        compiler_params=pltpu.CompilerParams(vmem_limit_bytes=60 << 20),
        name="cut",
    )(blocks)


def map_rows(weight_ref, cells_ref, first):
    coded = []
    for x in range(first, first + 8, 2):
        pair = [cells_ref[:, x + near].reshape(128, 128) for near in range(2)]
        mapped = jnp.dot(weight_ref[...], jnp.concatenate(pair, 1), preferred_element_type=jnp.float32)
        mapped = mapped * jnp.abs(mapped) * (mapped * mapped)
        coded += [mapped[:, :128], mapped[:, 128:]]
    turned = jnp.stack(coded, 0).transpose(1, 0, 2)
    return turned.reshape(BLOCKS, 8, 8, 128).astype(jnp.bfloat16)


def map_kernel(weight_ref, cells_ref, out_ref, kept_ref, block_ref, held_ref, fetched, stored):
    del kept_ref
    fetches, stores = [], []
    spans = [(0, EARLY % 16)] * (EARLY % 16 > 0) + [(first, 16) for first in range(EARLY % 16, EARLY, 16)]
    for part, (first, rows) in enumerate(spans):
        span = pl.ds(first, rows)
        fetches.append(pltpu.make_async_copy(cells_ref.at[:, span], block_ref.at[:, span], fetched.at[part]))
        fetches[part].start()
    for part, (start, rows) in enumerate(spans):
        fetches[part].wait()
        for first in range(start, start + rows, 8):
            held_ref[:, :, pl.ds(first, 8), :] = map_rows(weight_ref, block_ref, first)
        span = pl.ds(start, rows)
        stores.append(
            pltpu.make_async_copy(held_ref.at[:, :, span, :], out_ref.at[:, :, span, :], stored.at[part])
        )
        stores[part].start()
    for store in stores:
        store.wait()


def map_early(weight, cells):
    in_place = pl.BlockSpec(memory_space=pltpu.HBM)
    return pl.pallas_call(
        map_kernel,
        out_shape=[
            pltpu.HBM((BLOCKS, 8, EARLY, 128), jnp.bfloat16),
            pltpu.HBM((BLOCKS, EARLY, 8, 128), jnp.bfloat16),
        ],
        in_specs=[WHOLE, in_place],
        out_specs=[in_place] * 2,
        scratch_shapes=[
            pltpu.VMEM((BLOCKS, EARLY, 8, 128), jnp.bfloat16),
            pltpu.VMEM((BLOCKS, 8, EARLY, 128), jnp.bfloat16),
            pltpu.SemaphoreType.DMA((4,)),
            pltpu.SemaphoreType.DMA((4,)),
        ],
        input_output_aliases={1: 1},
        cost_estimate=pl.CostEstimate(flops=270_000_000, bytes_accessed=4_000_000, transcendentals=0),
        compiler_params=pltpu.CompilerParams(vmem_limit_bytes=10 << 20),
        name="map_early",
    )(weight, cells)[0]


def source_block(place_ref, k, h):
    return lax.bitwise_xor(place_ref[1], h) * 8 + lax.rem(place_ref[0] + (8 - k), 8)


def pack_kernel(place_ref, own_cells_ref, other_cells_ref, own_coef_ref, other_coef_ref, *letters):
    for k in range(8):
        target = lax.rem(place_ref[0] + k, 8)
        for h, (cells_ref, coef_ref) in enumerate(
            ((own_cells_ref, own_coef_ref), (other_cells_ref, other_coef_ref))
        ):
            letters[k][h, :LATE] = cells_ref[target]
            letters[k][h, LATE:] = coef_ref[...]


def pack(place, own_cells, other_cells, own_coef, other_coef):
    return pl.pallas_call(
        pack_kernel,
        out_shape=[jax.ShapeDtypeStruct((2, LATE + 4, 8, 128), jnp.bfloat16)] * 8,
        in_specs=[SCALARS] + [WHOLE] * 4,
        out_specs=[WHOLE] * 8,
        cost_estimate=pl.CostEstimate(flops=0, bytes_accessed=800_000, transcendentals=0),
        compiler_params=pltpu.CompilerParams(vmem_limit_bytes=4 << 20),
        name="pack",
    )(place, own_cells, other_cells, own_coef, other_coef)


def map_late_kernel(place_ref, weight_ref, *refs):
    letters, own_ref, other_ref, cells_ref, held_ref = refs[:8], refs[8], refs[9], refs[10], refs[11]
    for k in range(8):
        for h in range(2):
            cells_ref[source_block(place_ref, k, h)] = letters[k][h, :LATE]
    for first in range(0, LATE, 8):
        held_ref[:, :, pl.ds(first, 8), :] = map_rows(weight_ref, cells_ref, first)
    own_ref[...] = held_ref[pl.ds(place_ref[1] * 8, 8)]
    other_ref[...] = held_ref[pl.ds(8 - place_ref[1] * 8, 8)]


def map_late(place, weight, letters):
    return pl.pallas_call(
        map_late_kernel,
        out_shape=[jax.ShapeDtypeStruct((8, 8, LATE, 128), jnp.bfloat16)] * 2,
        in_specs=[SCALARS] + [WHOLE] * 9,
        out_specs=[WHOLE] * 2,
        scratch_shapes=[
            pltpu.VMEM((BLOCKS, LATE, 8, 128), jnp.bfloat16),
            pltpu.VMEM((BLOCKS, 8, LATE, 128), jnp.bfloat16),
        ],
        cost_estimate=pl.CostEstimate(flops=40_000_000, bytes_accessed=600_000, transcendentals=0),
        compiler_params=pltpu.CompilerParams(vmem_limit_bytes=6 << 20),
        name="map_late",
    )(place, weight, *letters)


def sort_kernel(place_ref, own_ref, other_ref, *letters):
    for k in range(8):
        target = lax.rem(place_ref[0] + k, 8)
        letters[k][0] = own_ref[target]
        letters[k][1] = other_ref[target]


def sort(place, own, other):
    return pl.pallas_call(
        sort_kernel,
        out_shape=[jax.ShapeDtypeStruct((2, 8, LATE, 128), jnp.bfloat16)] * 8,
        in_specs=[SCALARS] + [WHOLE] * 2,
        out_specs=[WHOLE] * 8,
        cost_estimate=pl.CostEstimate(flops=0, bytes_accessed=600_000, transcendentals=0),
        compiler_params=pltpu.CompilerParams(vmem_limit_bytes=4 << 20),
        name="sort",
    )(place, own, other)


def mix_kernel(place_ref, *refs):
    letters, weight_ref, out_ref, coef_ref = refs[:8], refs[8], refs[9], refs[10]
    for k in range(8):
        for h in range(2):
            for part in range(2):
                for side in range(2):
                    coded = letters[k][h, LATE + part * 2 + side]
                    coef_ref[k * 2 + h, part, :, pl.ds(side * 128, 128)] = decode(coded, COEF_SCALE)
    for o in range(8):
        real = jnp.zeros((8, 256), jnp.float32)
        imag = jnp.zeros((8, 256), jnp.float32)
        for k in range(8):
            for h in range(2):
                rows = pl.ds(pl.multiple_of(source_block(place_ref, k, h) * 8, 8), 8)
                weight_real = weight_ref[0, o, rows, :]
                weight_imag = weight_ref[1, o, rows, :]
                coef_real = coef_ref[k * 2 + h, 0]
                coef_imag = coef_ref[k * 2 + h, 1]
                real += coef_real * weight_real - coef_imag * weight_imag
                imag += coef_real * weight_imag + coef_imag * weight_real
        out_ref[0, pl.ds(o, 1), :] = jnp.sum(real, 0, keepdims=True)
        out_ref[1, pl.ds(o, 1), :] = jnp.sum(imag, 0, keepdims=True)


def mix(place, letters, spec_weight):
    return pl.pallas_call(
        mix_kernel,
        out_shape=jax.ShapeDtypeStruct((2, 8, 256), jnp.float32),
        in_specs=[SCALARS] + [WHOLE] * 9,
        out_specs=WHOLE,
        scratch_shapes=[pltpu.VMEM((BLOCKS, 2, 8, 256), jnp.float32)],
        cost_estimate=pl.CostEstimate(flops=5_000_000, bytes_accessed=3_000_000, transcendentals=0),
        compiler_params=pltpu.CompilerParams(vmem_limit_bytes=8 << 20),
        name="mix",
    )(place, *letters, spec_weight)


def inverse_kernel(me_ref, bias_ref, spec_ref, depth_ref, table_x_ref, waves_y_ref, out_ref, late_ref, *scratch):
    plane_ref, line_ref, table_ref, held_ref, stored = scratch
    row = lax.broadcasted_iota(jnp.int32, (256, 256), 0)
    lane = lax.broadcasted_iota(jnp.int32, (256, 256), 1)
    table_z = jnp.where(row // KEEP == lane % KEEP, jnp.concatenate([depth_ref[...]] * KEEP, 0), 0.0)
    real = exact_dot(spec_ref[:, 0].reshape(128, 256), table_z)
    imag = exact_dot(spec_ref[:, 1].reshape(128, 256), table_z)
    plane_real = (real[:, :128] - imag[:, 128:]).reshape(16, 8, 128)
    plane_imag = (imag[:, :128] + real[:, 128:]).reshape(16, 8, 128)
    for e in range(16):
        j = lax.bitwise_xor(me_ref[0], MIXED[e])
        plane_ref[j] = plane_real[e]
        plane_ref[16 + j] = plane_imag[e]
    for o in range(8):
        line = exact_dot(table_x_ref[...], plane_ref[:, o, :])
        line_ref[pl.ds(o * 128, 128), :] = jnp.concatenate([line[:128], line[128:]], 1)
    table_ref[...] = jnp.zeros_like(table_ref)
    for z in range(8):
        for part in range(2):
            table_ref[pl.ds(part * 128 + z * 16, 16), pl.ds(z * 128, 128)] = waves_y_ref[part]
    line_high, line_low = split(line_ref[...])
    stores = []
    for z in range(0, 8, 2):
        high, low = split(table_ref[:, z * 128 : (z + 2) * 128])
        field = jnp.dot(line_high, low, preferred_element_type=jnp.float32)
        field += jnp.dot(line_low, high, preferred_element_type=jnp.float32)
        field += jnp.dot(line_high, high, preferred_element_type=jnp.float32)
        for o in range(8):
            rows = slice(o * 128, (o + 1) * 128)
            for near in range(2):
                plane = field[rows, near * 128 : (near + 1) * 128] + bias_ref[o]
                for half in range(2):
                    block = (z + near) * 2 + half
                    held_ref[o, block] = plane[half * 64 : half * 64 + EARLY]
                    late_ref[o, block] = plane[half * 64 + EARLY : (half + 1) * 64]
        blocks = pl.ds(z * 2, 4)
        stores.append(pltpu.make_async_copy(held_ref.at[:, blocks], out_ref.at[:, blocks], stored.at[z // 2]))
        stores[z // 2].start()
    for store in stores:
        store.wait()


def inverse_transform(me, bias, spectrum, first_cell):
    cos_x, sin_x = plane_waves()
    table_x = jnp.asarray(
        np.concatenate([np.concatenate([cos_x.T, -sin_x.T], 1), np.concatenate([sin_x.T, cos_x.T], 1)], 0)
    )
    waves_y = jnp.asarray(np.stack([cos_x, -sin_x], 0))
    angle, row, lane = depth_angle(first_cell, (16, 256), lambda r, n: r, lambda r, n: n // 16 % 8)
    fold = jnp.where(row == 0, 1.0, 2.0) * (CELL_SCALE / GRID**3)
    depth = jnp.where(lane < 128, jnp.cos(angle), jnp.sin(angle)) * fold
    return pl.pallas_call(
        inverse_kernel,
        out_shape=[
            pltpu.HBM((8, BLOCKS, EARLY, 128), jnp.float32),
            jax.ShapeDtypeStruct((8, BLOCKS, LATE, 128), jnp.float32),
        ],
        in_specs=[SCALARS] * 2 + [WHOLE] * 4,
        out_specs=[pl.BlockSpec(memory_space=pltpu.HBM), WHOLE],
        scratch_shapes=[
            pltpu.VMEM((32, 8, 128), jnp.float32),
            pltpu.VMEM((1024, 256), jnp.float32),
            pltpu.VMEM((256, 1024), jnp.float32),
            pltpu.VMEM((8, BLOCKS, EARLY, 128), jnp.float32),
            pltpu.SemaphoreType.DMA((4,)),
        ],
        cost_estimate=pl.CostEstimate(flops=2_000_000_000, bytes_accessed=5_000_000, transcendentals=0),
        compiler_params=pltpu.CompilerParams(vmem_limit_bytes=16 << 20),
        name="inverse_transform",
    )(me, bias * CELL_SCALE, spectrum, depth, table_x, waves_y)


def activate(coded, inverse):
    total = decode(coded, 1.0) + inverse
    half = total * (0.5 / CELL_SCALE)
    return (half + half * lax.erf(total * (math.sqrt(0.5) / CELL_SCALE))).astype(jnp.bfloat16)


def finish_early_kernel(coded_ref, inverse_ref, out_ref, kept_ref, field_ref, done_ref, fetched, stored):
    del kept_ref
    parts = fetched.shape[0]
    span = BLOCKS // parts
    fetches, stores = [], []
    for part in range(parts):
        blocks = pl.ds(part * span, span)
        fetches.append(pltpu.make_async_copy(inverse_ref.at[:, blocks], field_ref.at[:, blocks], fetched.at[part]))
        fetches[part].start()
    for part in range(parts):
        fetches[part].wait()
        for o in range(8):
            for p in range(part * span, (part + 1) * span):
                done_ref[o, p] = activate(coded_ref[p, o], field_ref[o, p])
        blocks = pl.ds(part * span, span)
        target = out_ref.at[:, blocks, pl.ds(0, EARLY), :]
        stores.append(pltpu.make_async_copy(done_ref.at[:, blocks], target, stored.at[part]))
        stores[part].start()
    for store in stores:
        store.wait()


def finish_early(coded, inverse):
    parts = 8
    in_place = pl.BlockSpec(memory_space=pltpu.HBM)
    return pl.pallas_call(
        finish_early_kernel,
        out_shape=[
            pltpu.HBM((8, BLOCKS, 64, 128), jnp.bfloat16),
            pltpu.HBM((8, BLOCKS, EARLY, 128), jnp.float32),
        ],
        in_specs=[WHOLE, in_place],
        out_specs=[in_place] * 2,
        scratch_shapes=[
            pltpu.VMEM((8, BLOCKS, EARLY, 128), jnp.float32),
            pltpu.VMEM((8, BLOCKS, EARLY, 128), jnp.bfloat16),
            pltpu.SemaphoreType.DMA((parts,)),
            pltpu.SemaphoreType.DMA((parts,)),
        ],
        input_output_aliases={1: 1},
        cost_estimate=pl.CostEstimate(flops=30_000_000, bytes_accessed=8_000_000, transcendentals=0),
        compiler_params=pltpu.CompilerParams(vmem_limit_bytes=12 << 20),
        name="finish_early",
    )(coded, inverse)[0]


def finish_late_kernel(place_ref, inverse_ref, *refs):
    letters, out_ref, done_ref, stored = refs[:8], refs[9], refs[10], refs[11]
    for k in range(8):
        for h in range(2):
            block = source_block(place_ref, k, h)
            for o in range(8):
                done_ref[o, block] = activate(letters[k][h, o], inverse_ref[o, block])
    store = pltpu.make_async_copy(done_ref, out_ref.at[:, :, pl.ds(EARLY, LATE), :], stored)
    store.start()
    store.wait()


def finish_late(place, inverse, letters, partial):
    in_place = pl.BlockSpec(memory_space=pltpu.HBM)
    return pl.pallas_call(
        finish_late_kernel,
        out_shape=pltpu.HBM((8, BLOCKS, 64, 128), jnp.bfloat16),
        in_specs=[SCALARS] + [WHOLE] * 9 + [in_place],
        out_specs=in_place,
        scratch_shapes=[pltpu.VMEM((8, BLOCKS, LATE, 128), jnp.bfloat16), pltpu.SemaphoreType.DMA],
        input_output_aliases={10: 0},
        cost_estimate=pl.CostEstimate(flops=4_000_000, bytes_accessed=1_200_000, transcendentals=0),
        compiler_params=pltpu.CompilerParams(vmem_limit_bytes=6 << 20),
        name="finish_late",
    )(place, inverse, *letters, partial)


def z_letters(letters):
    arrived = [letters[0]]
    for k in range(1, 8):
        arrived.append(lax.ppermute(letters[k], "chan", chan_perm(0, k)))
    return arrived


def on_device(field, local_weight, bias, spec_weight):
    slab, chan = lax.axis_index("slab"), lax.axis_index("chan")
    first_cell = slab * 8
    x_hi = chan // 8
    place = jnp.stack([chan % 8, x_hi]).astype(jnp.int32)
    planes = field[0]
    blocks = planes.reshape(8, BLOCKS, 64, 128)
    weight = local_weight * jnp.bfloat16(CELL_SCALE)
    cells, own_cells, other_cells = cut(blocks)
    cells = lax.all_to_all(cells, "chan", 0, 0, tiled=True)
    other_cells = lax.ppermute(other_cells, "chan", chan_perm(1, 0))
    partial = forward_transform(planes, first_cell)
    owned = slab_sum(partial)
    own_coef = encode(owned, COEF_SCALE).reshape(2, 8, 2, 128).transpose(0, 2, 1, 3).reshape(4, 8, 128)
    other_coef = lax.ppermute(own_coef, "chan", chan_perm(1, 0))
    letters = pack(place, own_cells, other_cells, own_coef, other_coef)
    letters = z_letters(letters)
    coded = map_early(weight, cells)
    coded = lax.all_to_all(coded, "chan", 0, 0, tiled=True)
    mixed = mix(place, letters, spec_weight)
    own_late, other_late = map_late(place, weight, letters)
    other_late = lax.ppermute(other_late, "chan", chan_perm(1, 0))
    answers = sort(place, own_late, other_late)
    answers = z_letters(answers)
    spectrum = slab_gather(mixed)
    me = jnp.reshape(slab, (1,)).astype(jnp.int32)
    offset = lax.dynamic_slice_in_dim(bias, chan * 8, 8, 0)
    inverse, inverse_late = inverse_transform(me, offset, spectrum, first_cell)
    done = finish_early(coded, inverse)
    done = finish_late(place, inverse_late, answers, done)
    return done.reshape(1, 8, 8, 128, 128)


def solution(mesh):
    placed = (P(None, "chan", "slab", None, None), P(), P(), P(None, "chan", None, "slab"))
    return jax.shard_map(
        on_device,
        mesh=mesh,
        in_specs=placed,
        out_specs=P(None, "chan", "slab", None, None),
        check_vma=False,
    )
```

```python
import math

import jax
import jax.numpy as jnp
import numpy as np
from jax import lax
from jax.experimental import pallas as pl
from jax.experimental.pallas import tpu as pltpu
from jax.sharding import PartitionSpec as P


GRID = 128
KEEP = 16
BLOCKS = 16
LATE = 16
EARLY = 64 - LATE
CELL_SCALE = 2.0**20
COEF_SCALE = 2.0**6
WHOLE = pl.BlockSpec(memory_space=pltpu.VMEM)
SCALARS = pl.BlockSpec(memory_space=pltpu.SMEM)


def waves(freqs, positions):
    angle = 2.0 * math.pi * (freqs * positions % GRID).astype(np.float32) / np.float32(GRID)
    return np.cos(angle).astype(np.float32), np.sin(angle).astype(np.float32)


def plane_waves():
    index = np.arange(KEEP)
    freqs = np.where(index < KEEP // 2, index, index + GRID - KEEP)
    return waves(freqs[:, None], np.arange(GRID)[None, :])


def depth_angle(first_cell, shape, mode, cell):
    row = lax.broadcasted_iota(jnp.int32, shape, 0)
    lane = lax.broadcasted_iota(jnp.int32, shape, 1)
    turns = mode(row, lane) * (first_cell + cell(row, lane)) % GRID
    return 2.0 * math.pi * turns.astype(jnp.float32) / GRID, row, lane


def split(value):
    high = value.astype(jnp.bfloat16)
    return high, (value - high.astype(jnp.float32)).astype(jnp.bfloat16)


def exact_dot(left, right):
    left_high, left_low = split(left)
    right_high, right_low = split(right)
    total = jnp.dot(left_high, right_low, preferred_element_type=jnp.float32)
    total += jnp.dot(left_low, right_high, preferred_element_type=jnp.float32)
    return total + jnp.dot(left_high, right_high, preferred_element_type=jnp.float32)


def encode(value, scale):
    value = value * scale
    return (value * jnp.abs(value) * (value * value)).astype(jnp.bfloat16)


def decode(coded, scale):
    coded = coded.astype(jnp.float32)
    size = lax.rsqrt(lax.rsqrt(jnp.abs(coded)))
    if scale != 1.0:
        size = size * (1.0 / scale)
    return jnp.where(coded < 0, -size, size)


def slab_perm(dx, dy, dc):
    pairs = []
    for a in range(2):
        for b in range(4):
            for c in range(2):
                pairs.append(((a * 4 + b) * 2 + c, ((a ^ dx) * 4 + (b ^ dy)) * 2 + (c ^ dc)))
    return pairs


def chan_perm(dx, dz):
    return [(h * 8 + z, (h ^ dx) * 8 + (z + dz) % 8) for h in range(2) for z in range(8)]


def halve(value, axis, bit, perm):
    own = lax.dynamic_index_in_dim(value, bit, axis, keepdims=False)
    other = lax.dynamic_index_in_dim(value, 1 - bit, axis, keepdims=False)
    return own + lax.ppermute(other, "slab", perm)


def slab_sum(partial):
    me = lax.axis_index("slab")
    value = partial.reshape(2, 2, 2, 2, *partial.shape[1:])
    value = halve(value, 3, me % 2, slab_perm(0, 0, 1))
    value = halve(value, 1, me // 4 % 2, slab_perm(0, 2, 0))
    value = halve(value, 1, me // 2 % 2, slab_perm(0, 1, 0))
    return halve(value, 0, me // 8, slab_perm(1, 0, 0))


def slab_gather(value):
    value = value[None]
    for step in ((1, 0, 0), (0, 1, 0), (0, 2, 0), (0, 0, 1)):
        other = lax.ppermute(value, "slab", slab_perm(*step))
        value = jnp.concatenate([value, other], 0)
    return value


MIXED = tuple((e & 1) * 8 | (e >> 1 & 1) * 2 | (e >> 2 & 1) * 4 | e >> 3 for e in range(16))


def forward_kernel(field_ref, table_x_ref, table_y_ref, depth_ref, out_ref, wave_ref, table_z_ref):
    table_y = table_y_ref[...]
    lane = lax.broadcasted_iota(jnp.int32, (KEEP, 512), 1)
    row = lax.broadcasted_iota(jnp.int32, (KEEP, 512), 0)
    same_mode = lane // KEEP % KEEP == row
    for z in range(8):
        sections = []
        for c in range(8):
            section = jnp.dot(table_x_ref[...], field_ref[c, z], preferred_element_type=jnp.float32)
            sections.append(jnp.concatenate([section[:KEEP], section[KEEP:]], 1))
        wave_ref[:, pl.ds(z * 32, 32)] = exact_dot(jnp.concatenate(sections, 0), table_y)
        for part in range(2):
            rows = pl.ds(z * 32 + part * KEEP, KEEP)
            depth = jnp.broadcast_to(depth_ref[pl.ds(z * 2 + part, 1), :], (KEEP, 512))
            table_z_ref[rows, :] = jnp.where(same_mode, depth, 0.0)
    coefs = exact_dot(wave_ref[...], table_z_ref[...]).reshape(8, KEEP, 512).transpose(1, 0, 2)
    out_ref[:, 0] = coefs[:, :, :256]
    out_ref[:, 1] = coefs[:, :, 256:]


def forward_transform(field, first_cell):
    cos_x, sin_x = plane_waves()
    table_x = jnp.asarray(np.concatenate([cos_x, -sin_x], 0)).astype(jnp.bfloat16)
    table_y = jnp.asarray(
        np.concatenate([np.concatenate([cos_x.T, -sin_x.T], 1), np.concatenate([sin_x.T, cos_x.T], 1)], 0)
    )
    angle, row, lane = depth_angle(first_cell, (16, 512), lambda r, n: n % 16, lambda r, n: r // 2)
    from_part, to_part = row % 2, lane // 256
    turned = jnp.where(from_part == 1, jnp.sin(angle), -jnp.sin(angle))
    depth = jnp.where(from_part == to_part, jnp.cos(angle), turned)
    return pl.pallas_call(
        forward_kernel,
        out_shape=jax.ShapeDtypeStruct((KEEP, 2, 8, 256), jnp.float32),
        in_specs=[WHOLE] * 4,
        out_specs=WHOLE,
        scratch_shapes=[pltpu.VMEM((128, 256), jnp.float32), pltpu.VMEM((256, 512), jnp.float32)],
        cost_estimate=pl.CostEstimate(flops=200_000_000, bytes_accessed=3_000_000, transcendentals=0),
        compiler_params=pltpu.CompilerParams(vmem_limit_bytes=12 << 20),
        name="forward_transform",
    )(field, table_x, table_y, depth)


def cut_kernel(field_ref, early_ref, own_ref, other_ref, block_ref, turned_ref, late_ref, fetched, stored, parted):
    x_hi = lax.shift_right_logical(lax.axis_index("chan"), 3)
    parts = fetched.shape[0]
    span = BLOCKS // parts
    fetches, stores = [], []
    for part in range(parts):
        blocks = pl.ds(part * span, span)
        fetches.append(pltpu.make_async_copy(field_ref.at[:, blocks], block_ref.at[:, blocks], fetched.at[part]))
        fetches[part].start()
    for part in range(parts):
        fetches[part].wait()
        for p in range(part * span, (part + 1) * span):
            block = block_ref[:, p].astype(jnp.float32)
            turned = block.transpose(1, 0, 2).astype(jnp.bfloat16)
            turned_ref[p] = turned[:EARLY]
            late_ref[p // 8, p % 8] = turned[EARLY:]
        blocks = pl.ds(part * span, span)
        stores.append(pltpu.make_async_copy(turned_ref.at[blocks], early_ref.at[blocks], stored.at[part]))
        stores[part].start()
        if (part + 1) % (parts // 2) == 0:
            half = part // (parts // 2)
            for target, side in ((own_ref, half), (other_ref, 1 - half)):

                @pl.when(x_hi == side)
                def _():
                    pltpu.make_async_copy(late_ref.at[half], target, parted.at[half]).start()

    for half in range(2):
        stores.append(pltpu.make_async_copy(late_ref.at[half], own_ref, parted.at[half]))
    for store in stores:
        store.wait()


def cut(blocks):
    parts = 8
    in_place = pl.BlockSpec(memory_space=pltpu.HBM)
    return pl.pallas_call(
        cut_kernel,
        out_shape=[pltpu.HBM((BLOCKS, EARLY, 8, 128), jnp.bfloat16)]
        + [pltpu.HBM((8, LATE, 8, 128), jnp.bfloat16)] * 2,
        in_specs=[in_place],
        out_specs=[in_place] * 3,
        scratch_shapes=[
            pltpu.VMEM((8, BLOCKS, 64, 128), jnp.bfloat16),
            pltpu.VMEM((BLOCKS, EARLY, 8, 128), jnp.bfloat16),
            pltpu.VMEM((2, 8, LATE, 8, 128), jnp.bfloat16),
            pltpu.SemaphoreType.DMA((parts,)),
            pltpu.SemaphoreType.DMA((parts,)),
            pltpu.SemaphoreType.DMA((2,)),
        ],
        cost_estimate=pl.CostEstimate(flops=1_000_000, bytes_accessed=4_000_000, transcendentals=0),
        compiler_params=pltpu.CompilerParams(vmem_limit_bytes=60 << 20),
        name="cut",
    )(blocks)


def map_rows(weight_ref, cells_ref, first):
    coded = []
    for x in range(first, first + 8, 2):
        pair = [cells_ref[:, x + near].reshape(128, 128) for near in range(2)]
        mapped = jnp.dot(weight_ref[...], jnp.concatenate(pair, 1), preferred_element_type=jnp.float32)
        mapped = mapped * jnp.abs(mapped) * (mapped * mapped)
        coded += [mapped[:, :128], mapped[:, 128:]]
    turned = jnp.stack(coded, 0).transpose(1, 0, 2)
    return turned.reshape(BLOCKS, 8, 8, 128).astype(jnp.bfloat16)


def map_kernel(weight_ref, cells_ref, out_ref, kept_ref, block_ref, held_ref, fetched, stored):
    del kept_ref
    fetches, stores = [], []
    spans = [(0, EARLY % 16)] * (EARLY % 16 > 0) + [(first, 16) for first in range(EARLY % 16, EARLY, 16)]
    for part, (first, rows) in enumerate(spans):
        span = pl.ds(first, rows)
        fetches.append(pltpu.make_async_copy(cells_ref.at[:, span], block_ref.at[:, span], fetched.at[part]))
        fetches[part].start()
    for part, (start, rows) in enumerate(spans):
        fetches[part].wait()
        for first in range(start, start + rows, 8):
            held_ref[:, :, pl.ds(first, 8), :] = map_rows(weight_ref, block_ref, first)
        span = pl.ds(start, rows)
        stores.append(
            pltpu.make_async_copy(held_ref.at[:, :, span, :], out_ref.at[:, :, span, :], stored.at[part])
        )
        stores[part].start()
    for store in stores:
        store.wait()


def map_early(weight, cells):
    in_place = pl.BlockSpec(memory_space=pltpu.HBM)
    return pl.pallas_call(
        map_kernel,
        out_shape=[
            pltpu.HBM((BLOCKS, 8, EARLY, 128), jnp.bfloat16),
            pltpu.HBM((BLOCKS, EARLY, 8, 128), jnp.bfloat16),
        ],
        in_specs=[WHOLE, in_place],
        out_specs=[in_place] * 2,
        scratch_shapes=[
            pltpu.VMEM((BLOCKS, EARLY, 8, 128), jnp.bfloat16),
            pltpu.VMEM((BLOCKS, 8, EARLY, 128), jnp.bfloat16),
            pltpu.SemaphoreType.DMA((4,)),
            pltpu.SemaphoreType.DMA((4,)),
        ],
        input_output_aliases={1: 1},
        cost_estimate=pl.CostEstimate(flops=270_000_000, bytes_accessed=4_000_000, transcendentals=0),
        compiler_params=pltpu.CompilerParams(vmem_limit_bytes=10 << 20),
        name="map_early",
    )(weight, cells)[0]


def source_block(place_ref, k, h):
    return lax.bitwise_xor(place_ref[1], h) * 8 + lax.rem(place_ref[0] + (8 - k), 8)


def pack_kernel(place_ref, own_cells_ref, other_cells_ref, own_coef_ref, other_coef_ref, *letters):
    for k in range(8):
        target = lax.rem(place_ref[0] + k, 8)
        for h, (cells_ref, coef_ref) in enumerate(
            ((own_cells_ref, own_coef_ref), (other_cells_ref, other_coef_ref))
        ):
            letters[k][h, :LATE] = cells_ref[target]
            letters[k][h, LATE:] = coef_ref[...]


def pack(place, own_cells, other_cells, own_coef, other_coef):
    return pl.pallas_call(
        pack_kernel,
        out_shape=[jax.ShapeDtypeStruct((2, LATE + 4, 8, 128), jnp.bfloat16)] * 8,
        in_specs=[SCALARS] + [WHOLE] * 4,
        out_specs=[WHOLE] * 8,
        cost_estimate=pl.CostEstimate(flops=0, bytes_accessed=800_000, transcendentals=0),
        compiler_params=pltpu.CompilerParams(vmem_limit_bytes=4 << 20),
        name="pack",
    )(place, own_cells, other_cells, own_coef, other_coef)


def map_late_kernel(place_ref, weight_ref, *refs):
    letters, own_ref, other_ref, cells_ref, held_ref = refs[:8], refs[8], refs[9], refs[10], refs[11]
    for k in range(8):
        for h in range(2):
            cells_ref[source_block(place_ref, k, h)] = letters[k][h, :LATE]
    for first in range(0, LATE, 8):
        held_ref[:, :, pl.ds(first, 8), :] = map_rows(weight_ref, cells_ref, first)
    own_ref[...] = held_ref[pl.ds(place_ref[1] * 8, 8)]
    other_ref[...] = held_ref[pl.ds(8 - place_ref[1] * 8, 8)]


def map_late(place, weight, letters):
    return pl.pallas_call(
        map_late_kernel,
        out_shape=[jax.ShapeDtypeStruct((8, 8, LATE, 128), jnp.bfloat16)] * 2,
        in_specs=[SCALARS] + [WHOLE] * 9,
        out_specs=[WHOLE] * 2,
        scratch_shapes=[
            pltpu.VMEM((BLOCKS, LATE, 8, 128), jnp.bfloat16),
            pltpu.VMEM((BLOCKS, 8, LATE, 128), jnp.bfloat16),
        ],
        cost_estimate=pl.CostEstimate(flops=40_000_000, bytes_accessed=600_000, transcendentals=0),
        compiler_params=pltpu.CompilerParams(vmem_limit_bytes=6 << 20),
        name="map_late",
    )(place, weight, *letters)


def sort_kernel(place_ref, own_ref, other_ref, *letters):
    for k in range(8):
        target = lax.rem(place_ref[0] + k, 8)
        letters[k][0] = own_ref[target]
        letters[k][1] = other_ref[target]


def sort(place, own, other):
    return pl.pallas_call(
        sort_kernel,
        out_shape=[jax.ShapeDtypeStruct((2, 8, LATE, 128), jnp.bfloat16)] * 8,
        in_specs=[SCALARS] + [WHOLE] * 2,
        out_specs=[WHOLE] * 8,
        cost_estimate=pl.CostEstimate(flops=0, bytes_accessed=600_000, transcendentals=0),
        compiler_params=pltpu.CompilerParams(vmem_limit_bytes=4 << 20),
        name="sort",
    )(place, own, other)


def mix_kernel(place_ref, *refs):
    letters, weight_ref, out_ref, coef_ref = refs[:8], refs[8], refs[9], refs[10]
    for k in range(8):
        for h in range(2):
            for part in range(2):
                for side in range(2):
                    coded = letters[k][h, LATE + part * 2 + side]
                    coef_ref[k * 2 + h, part, :, pl.ds(side * 128, 128)] = decode(coded, COEF_SCALE)
    for o in range(8):
        real = jnp.zeros((8, 256), jnp.float32)
        imag = jnp.zeros((8, 256), jnp.float32)
        for k in range(8):
            for h in range(2):
                rows = pl.ds(pl.multiple_of(source_block(place_ref, k, h) * 8, 8), 8)
                weight_real = weight_ref[0, o, rows, :]
                weight_imag = weight_ref[1, o, rows, :]
                coef_real = coef_ref[k * 2 + h, 0]
                coef_imag = coef_ref[k * 2 + h, 1]
                real += coef_real * weight_real - coef_imag * weight_imag
                imag += coef_real * weight_imag + coef_imag * weight_real
        out_ref[0, pl.ds(o, 1), :] = jnp.sum(real, 0, keepdims=True)
        out_ref[1, pl.ds(o, 1), :] = jnp.sum(imag, 0, keepdims=True)


def mix(place, letters, spec_weight):
    return pl.pallas_call(
        mix_kernel,
        out_shape=jax.ShapeDtypeStruct((2, 8, 256), jnp.float32),
        in_specs=[SCALARS] + [WHOLE] * 9,
        out_specs=WHOLE,
        scratch_shapes=[pltpu.VMEM((BLOCKS, 2, 8, 256), jnp.float32)],
        cost_estimate=pl.CostEstimate(flops=5_000_000, bytes_accessed=3_000_000, transcendentals=0),
        compiler_params=pltpu.CompilerParams(vmem_limit_bytes=8 << 20),
        name="mix",
    )(place, *letters, spec_weight)


def inverse_kernel(me_ref, bias_ref, spec_ref, depth_ref, table_x_ref, waves_y_ref, out_ref, late_ref, *scratch):
    plane_ref, line_ref, table_ref, held_ref, stored = scratch
    row = lax.broadcasted_iota(jnp.int32, (256, 256), 0)
    lane = lax.broadcasted_iota(jnp.int32, (256, 256), 1)
    table_z = jnp.where(row // KEEP == lane % KEEP, jnp.concatenate([depth_ref[...]] * KEEP, 0), 0.0)
    real = exact_dot(spec_ref[:, 0].reshape(128, 256), table_z)
    imag = exact_dot(spec_ref[:, 1].reshape(128, 256), table_z)
    plane_real = (real[:, :128] - imag[:, 128:]).reshape(16, 8, 128)
    plane_imag = (imag[:, :128] + real[:, 128:]).reshape(16, 8, 128)
    for e in range(16):
        j = lax.bitwise_xor(me_ref[0], MIXED[e])
        plane_ref[j] = plane_real[e]
        plane_ref[16 + j] = plane_imag[e]
    for o in range(8):
        line = exact_dot(table_x_ref[...], plane_ref[:, o, :])
        line_ref[pl.ds(o * 128, 128), :] = jnp.concatenate([line[:128], line[128:]], 1)
    table_ref[...] = jnp.zeros_like(table_ref)
    for z in range(8):
        for part in range(2):
            table_ref[pl.ds(part * 128 + z * 16, 16), pl.ds(z * 128, 128)] = waves_y_ref[part]
    line_high, line_low = split(line_ref[...])
    stores = []
    for z in range(0, 8, 2):
        high, low = split(table_ref[:, z * 128 : (z + 2) * 128])
        field = jnp.dot(line_high, low, preferred_element_type=jnp.float32)
        field += jnp.dot(line_low, high, preferred_element_type=jnp.float32)
        field += jnp.dot(line_high, high, preferred_element_type=jnp.float32)
        for o in range(8):
            rows = slice(o * 128, (o + 1) * 128)
            for near in range(2):
                plane = field[rows, near * 128 : (near + 1) * 128] + bias_ref[o]
                for half in range(2):
                    block = (z + near) * 2 + half
                    held_ref[o, block] = plane[half * 64 : half * 64 + EARLY]
                    late_ref[o, block] = plane[half * 64 + EARLY : (half + 1) * 64]
        blocks = pl.ds(z * 2, 4)
        stores.append(pltpu.make_async_copy(held_ref.at[:, blocks], out_ref.at[:, blocks], stored.at[z // 2]))
        stores[z // 2].start()
    for store in stores:
        store.wait()


def inverse_transform(me, bias, spectrum, first_cell):
    cos_x, sin_x = plane_waves()
    table_x = jnp.asarray(
        np.concatenate([np.concatenate([cos_x.T, -sin_x.T], 1), np.concatenate([sin_x.T, cos_x.T], 1)], 0)
    )
    waves_y = jnp.asarray(np.stack([cos_x, -sin_x], 0))
    angle, row, lane = depth_angle(first_cell, (16, 256), lambda r, n: r, lambda r, n: n // 16 % 8)
    fold = jnp.where(row == 0, 1.0, 2.0) * (CELL_SCALE / GRID**3)
    depth = jnp.where(lane < 128, jnp.cos(angle), jnp.sin(angle)) * fold
    return pl.pallas_call(
        inverse_kernel,
        out_shape=[
            pltpu.HBM((8, BLOCKS, EARLY, 128), jnp.float32),
            jax.ShapeDtypeStruct((8, BLOCKS, LATE, 128), jnp.float32),
        ],
        in_specs=[SCALARS] * 2 + [WHOLE] * 4,
        out_specs=[pl.BlockSpec(memory_space=pltpu.HBM), WHOLE],
        scratch_shapes=[
            pltpu.VMEM((32, 8, 128), jnp.float32),
            pltpu.VMEM((1024, 256), jnp.float32),
            pltpu.VMEM((256, 1024), jnp.float32),
            pltpu.VMEM((8, BLOCKS, EARLY, 128), jnp.float32),
            pltpu.SemaphoreType.DMA((4,)),
        ],
        cost_estimate=pl.CostEstimate(flops=2_000_000_000, bytes_accessed=5_000_000, transcendentals=0),
        compiler_params=pltpu.CompilerParams(vmem_limit_bytes=16 << 20),
        name="inverse_transform",
    )(me, bias * CELL_SCALE, spectrum, depth, table_x, waves_y)


def activate(coded, inverse):
    total = decode(coded, 1.0) + inverse
    half = total * (0.5 / CELL_SCALE)
    return (half + half * lax.erf(total * (math.sqrt(0.5) / CELL_SCALE))).astype(jnp.bfloat16)


def finish_early_kernel(coded_ref, inverse_ref, out_ref, kept_ref, field_ref, done_ref, fetched, stored):
    del kept_ref
    parts = fetched.shape[0]
    span = BLOCKS // parts
    fetches, stores = [], []
    for part in range(parts):
        blocks = pl.ds(part * span, span)
        fetches.append(pltpu.make_async_copy(inverse_ref.at[:, blocks], field_ref.at[:, blocks], fetched.at[part]))
        fetches[part].start()
    for part in range(parts):
        fetches[part].wait()
        for o in range(8):
            for p in range(part * span, (part + 1) * span):
                done_ref[o, p] = activate(coded_ref[p, o], field_ref[o, p])
        blocks = pl.ds(part * span, span)
        target = out_ref.at[:, blocks, pl.ds(0, EARLY), :]
        stores.append(pltpu.make_async_copy(done_ref.at[:, blocks], target, stored.at[part]))
        stores[part].start()
    for store in stores:
        store.wait()


def finish_early(coded, inverse):
    parts = 8
    in_place = pl.BlockSpec(memory_space=pltpu.HBM)
    return pl.pallas_call(
        finish_early_kernel,
        out_shape=[
            pltpu.HBM((8, BLOCKS, 64, 128), jnp.bfloat16),
            pltpu.HBM((8, BLOCKS, EARLY, 128), jnp.float32),
        ],
        in_specs=[WHOLE, in_place],
        out_specs=[in_place] * 2,
        scratch_shapes=[
            pltpu.VMEM((8, BLOCKS, EARLY, 128), jnp.float32),
            pltpu.VMEM((8, BLOCKS, EARLY, 128), jnp.bfloat16),
            pltpu.SemaphoreType.DMA((parts,)),
            pltpu.SemaphoreType.DMA((parts,)),
        ],
        input_output_aliases={1: 1},
        cost_estimate=pl.CostEstimate(flops=30_000_000, bytes_accessed=8_000_000, transcendentals=0),
        compiler_params=pltpu.CompilerParams(vmem_limit_bytes=12 << 20),
        name="finish_early",
    )(coded, inverse)[0]


def finish_late_kernel(place_ref, inverse_ref, *refs):
    letters, out_ref, done_ref, stored = refs[:8], refs[9], refs[10], refs[11]
    for k in range(8):
        for h in range(2):
            block = source_block(place_ref, k, h)
            for o in range(8):
                done_ref[o, block] = activate(letters[k][h, o], inverse_ref[o, block])
    store = pltpu.make_async_copy(done_ref, out_ref.at[:, :, pl.ds(EARLY, LATE), :], stored)
    store.start()
    store.wait()


def finish_late(place, inverse, letters, partial):
    in_place = pl.BlockSpec(memory_space=pltpu.HBM)
    return pl.pallas_call(
        finish_late_kernel,
        out_shape=pltpu.HBM((8, BLOCKS, 64, 128), jnp.bfloat16),
        in_specs=[SCALARS] + [WHOLE] * 9 + [in_place],
        out_specs=in_place,
        scratch_shapes=[pltpu.VMEM((8, BLOCKS, LATE, 128), jnp.bfloat16), pltpu.SemaphoreType.DMA],
        input_output_aliases={10: 0},
        cost_estimate=pl.CostEstimate(flops=4_000_000, bytes_accessed=1_200_000, transcendentals=0),
        compiler_params=pltpu.CompilerParams(vmem_limit_bytes=6 << 20),
        name="finish_late",
    )(place, inverse, *letters, partial)


def z_letters(letters):
    arrived = [letters[0]]
    for k in range(1, 8):
        arrived.append(lax.ppermute(letters[k], "chan", chan_perm(0, k)))
    return arrived


def on_device(field, local_weight, bias, spec_weight):
    slab, chan = lax.axis_index("slab"), lax.axis_index("chan")
    first_cell = slab * 8
    x_hi = chan // 8
    place = jnp.stack([chan % 8, x_hi]).astype(jnp.int32)
    planes = field[0]
    blocks = planes.reshape(8, BLOCKS, 64, 128)
    weight = local_weight * jnp.bfloat16(CELL_SCALE)
    cells, own_cells, other_cells = cut(blocks)
    cells = lax.all_to_all(cells, "chan", 0, 0, tiled=True)
    other_cells = lax.ppermute(other_cells, "chan", chan_perm(1, 0))
    partial = forward_transform(planes, first_cell)
    owned = slab_sum(partial)
    own_coef = encode(owned, COEF_SCALE).reshape(2, 8, 2, 128).transpose(0, 2, 1, 3).reshape(4, 8, 128)
    other_coef = lax.ppermute(own_coef, "chan", chan_perm(1, 0))
    letters = pack(place, own_cells, other_cells, own_coef, other_coef)
    letters = z_letters(letters)
    coded = map_early(weight, cells)
    coded = lax.all_to_all(coded, "chan", 0, 0, tiled=True)
    mixed = mix(place, letters, spec_weight)
    own_late, other_late = map_late(place, weight, letters)
    other_late = lax.ppermute(other_late, "chan", chan_perm(1, 0))
    answers = sort(place, own_late, other_late)
    answers = z_letters(answers)
    spectrum = slab_gather(mixed)
    me = jnp.reshape(slab, (1,)).astype(jnp.int32)
    offset = lax.dynamic_slice_in_dim(bias, chan * 8, 8, 0)
    inverse, inverse_late = inverse_transform(me, offset, spectrum, first_cell)
    done = finish_early(coded, inverse)
    done = finish_late(place, inverse_late, answers, done)
    return done.reshape(1, 8, 8, 128, 128)


def solution(mesh):
    placed = (P(None, "chan", "slab", None, None), P(), P(), P(None, "chan", None, "slab"))
    return jax.shard_map(
        on_device,
        mesh=mesh,
        in_specs=placed,
        out_specs=P(None, "chan", "slab", None, None),
        check_vma=False,
    )
```
